128 devices in a mesh: row: 16 (over z, x), col: 8 (over y, core).
Axes of the slice: x: 4, y: 4, z: 4, core: 2. Of those that a mesh axis runs over, the one named last changes fastest.
Arguments:
- features: bfloat16 [65536, 256], P(('col', 'row')), may hold values from -6 to 6
- adjacency: bfloat16 [512, 8, 12, 128, 128], P('row', 'col'), may hold values from 0 to 0.023925781
- block_cols: int32 [512, 8, 12], P('row', 'col'), may hold values from 0 to 63, as said below
- block_live: int32 [512, 8], P('row', 'col'), may hold values from 1 to 12, as said below
- weight: bfloat16 [256, 256], replicated, may hold values from -0.375 to 0.375
- bias: float32 [256], replicated, may hold values from -3 to 3
- upstream: bfloat16 [65536, 256], P(('row', 'col')), may hold values from -6 to 6
Outputs:
- activations: bfloat16 [65536, 256], P(('row', 'col'))
- feature_grad: bfloat16 [65536, 256], P(('col', 'row'))
- weight_grad: float32 [256, 256], replicated
- bias_grad: float32 [256], replicated
The draws below stay inside these ranges and needn't reach their ends.
Inputs may be any that keep to these rules, and one draw needn't show every extreme that they name: `block_cols`: the live slots of one block row in one column tile name distinct column blocks of that tile. Slots k with k < block_live[i, c] are live; the other slots of block_cols and adjacency are ignored. Some entry equals 12.
All inputs are finite; a program needn't handle non-finite values.
Results may differ from the reference program's by a relative error of at most 0.014.
Values may be sent and summed in bfloat16 or wider, within the bound.
A program may use at most 256 MiB of HBM per device.

```python
import jax
import jax.numpy as jnp
from jax import lax

F = 256
BS = 128
BR = 32
KB = 12
NBR = 512
BCOL = 64
N = 65536
N_ROW = 16
N_COL = 8


def draw_block_cols(key, part):
    tile_blocks = BR * N_ROW // N_COL
    scores = jax.random.randint(key, (BR * N_ROW, N_COL, tile_blocks), 0, 1 << 20) * tile_blocks
    scores = scores + jnp.arange(tile_blocks, dtype=jnp.int32)
    ranked = jnp.argsort(scores, axis=-1)
    return ranked[:, :, :KB].astype(jnp.int32)


def draw_block_live(key, part):
    heavy_key = jax.random.fold_in(key, 11)
    base_key = jax.random.fold_in(key, 12)
    place_key = jax.random.fold_in(key, 13)
    heavy_factor = jax.random.randint(heavy_key, (N_ROW, 1, N_COL), 0, 4)
    base_count = jax.random.randint(base_key, (N_ROW, BR, N_COL), 1, max(KB // 4, 1) + 1)
    live_count = jnp.minimum(base_count * (1 + heavy_factor), KB).reshape(-1)
    position = jax.random.randint(place_key, (), 0, BR * N_ROW * N_COL)
    live_count = live_count.at[position].set(KB)
    return live_count.reshape(BR * N_ROW, N_COL).astype(jnp.int32)


def shard_levels(key, shape, pieces, low, top_value):
    level, own = 1.0, jax.random.fold_in(key, 6)
    for dim, blocks in pieces:
        heights = jnp.exp(jax.random.uniform(jax.random.fold_in(own, dim), (blocks,), jnp.float32, low / len(pieces), top_value / len(pieces)))
        level = level * jnp.repeat(heights, shape[dim] // blocks).reshape([-1 if axis == dim else 1 for axis in range(len(shape))])
    return level


def noise(own_key, extent, deviation, reach, split=(), kind=jnp.bfloat16):
    entries = deviation * jax.random.normal(own_key, extent, jnp.float32)
    if split:
        entries = entries * shard_levels(own_key, extent, split, -0.22, 0.18)
    return jnp.clip(entries, -reach, reach).astype(kind)


def setup_inputs(seed: int = 0) -> dict:
    keys = jax.random.split(jax.random.key(seed), 8)
    return {
        "features": noise(keys[0], (N, F), 1.0, 6.0, ((0, 128),)),
        "adjacency": jnp.clip(0.023925781 * jax.random.uniform(keys[1], (NBR, N_COL, KB, BS, BS), jnp.float32) ** shard_levels(keys[1], (NBR, N_COL, KB, BS, BS), ((0, 16), (1, 8)), -0.2, 0.2), 0.0, 0.023925781).astype(jnp.bfloat16),
        "block_cols": draw_block_cols(jax.random.fold_in(keys[7], 71), 0),
        "block_live": draw_block_live(jax.random.fold_in(keys[7], 71), 0),
        "weight": noise(keys[4], (F, F), F ** -0.5, 0.375),
        "bias": noise(keys[5], (F,), 0.5, 3.0, (), jnp.float32),
        "upstream": noise(keys[6], (N, F), 1.0, 6.0, ((0, 128),)),
    }


def reference(features, adjacency, block_cols, block_live, weight, bias, upstream):
    panels = features.reshape(N_COL, BCOL, BS, F)
    slot_ids = jnp.arange(KB)
    tile_ids = jnp.arange(N_COL)[:, None]

    def row_product(inputs):
        blocks, column_ids, live_count = inputs
        picked = panels[tile_ids, column_ids].astype(jnp.float32)
        live_mask = slot_ids[None, :] < live_count[:, None]
        picked = jnp.where(live_mask[:, :, None, None], picked, jnp.float32(0.0))
        return jnp.einsum("ckab,ckbf->af", blocks.astype(jnp.float32), picked)

    aggregated = lax.map(row_product, (adjacency, block_cols, block_live))
    aggregated = aggregated.reshape(N, F).astype(jnp.bfloat16)
    preact = jnp.dot(aggregated, weight, preferred_element_type=jnp.float32) + bias
    sigmoid_pre = jax.nn.sigmoid(preact)
    activations = (preact * sigmoid_pre).astype(jnp.bfloat16)
    derivative = sigmoid_pre * (1.0 + preact * (1.0 - sigmoid_pre))
    grad_pre = (upstream.astype(jnp.float32) * derivative).astype(jnp.bfloat16)
    weight_grad = jnp.dot(aggregated.T, grad_pre, preferred_element_type=jnp.float32)
    bias_grad = jnp.sum(grad_pre.astype(jnp.float32), axis=0)
    grad_agg = jnp.dot(grad_pre, weight.T, preferred_element_type=jnp.float32).astype(jnp.bfloat16)
    grad_blocks = grad_agg.reshape(NBR, BS, F)

    def spread(totals, inputs):
        blocks, column_ids, live_count, grad_rows = inputs
        contrib = jnp.einsum("ckab,af->ckbf", blocks.astype(jnp.float32), grad_rows.astype(jnp.float32))
        live_mask = slot_ids[None, :] < live_count[:, None]
        contrib = jnp.where(live_mask[:, :, None, None], contrib, jnp.float32(0.0))
        totals = totals.at[tile_ids, column_ids].add(contrib)
        return totals, None

    totals = jnp.zeros((N_COL, BCOL, BS, F), jnp.float32)
    totals, _ = lax.scan(spread, totals, (adjacency, block_cols, block_live, grad_blocks))
    feature_grad = totals.reshape(N, F).astype(jnp.bfloat16)
    return activations, feature_grad, weight_grad, bias_grad
```

```python
import jax
import jax.numpy as jnp
from jax import lax
from jax.experimental import pallas as pl
from jax.experimental.pallas import tpu as pltpu
from jax.sharding import PartitionSpec as P


def forward_body(cols_ref, adj_ref, panel_ref, out_ref):
    i = pl.program_id(0)
    slots = adj_ref.shape[1]
    total = None
    for k in range(0, slots, 2):
        left = jnp.concatenate([adj_ref[0, k], adj_ref[0, k + 1]], axis=1)
        blocks = []
        for s in (k, k + 1):
            j = cols_ref[i * slots + s]
            block = panel_ref[jnp.minimum(j, panel_ref.shape[0] - 1)]
            blocks.append(jnp.where(j < panel_ref.shape[0], block, jnp.zeros_like(block)))
        right = jnp.concatenate(blocks, axis=0)
        part = jnp.dot(left, right, preferred_element_type=jnp.float32)
        total = part if total is None else total + part
    out_ref[0] = total.astype(out_ref.dtype)


def backward_body(cols_ref, adj_ref, grad_ref, out_ref, acc_ref):
    i = pl.program_id(0)
    slots = adj_ref.shape[1]
    size = adj_ref.shape[3]

    @pl.when(i == 0)
    def _():
        acc_ref[...] = jnp.zeros_like(acc_ref)

    turned = grad_ref[0].T
    for k in range(0, slots, 2):
        right = jnp.concatenate([adj_ref[0, k], adj_ref[0, k + 1]], axis=1)
        part = jnp.dot(turned, right, preferred_element_type=jnp.float32)
        for s in (0, 1):
            j = cols_ref[i * slots + k + s]
            acc_ref[j] += part[:, s * size : (s + 1) * size]

    @pl.when(i == pl.num_programs(0) - 1)
    def _():
        @pl.loop(0, out_ref.shape[0])
        def _(j):
            out_ref[j] = acc_ref[j].astype(out_ref.dtype)


def forward_product(cols, adj, panel):
    rows, slots, size, _ = adj.shape
    width = panel.shape[2]
    return pl.pallas_call(
        forward_body,
        out_shape=jax.ShapeDtypeStruct((rows, size, width), jnp.bfloat16),
        grid_spec=pltpu.PrefetchScalarGridSpec(
            num_scalar_prefetch=1,
            grid=(rows,),
            in_specs=[
                pl.BlockSpec((1, slots, size, size), lambda i, c: (i, 0, 0, 0)),
                pl.BlockSpec(panel.shape, lambda i, c: (0, 0, 0), pipeline_mode=pl.Buffered(1)),
            ],
            out_specs=pl.BlockSpec((1, size, width), lambda i, c: (i, 0, 0)),
        ),
        compiler_params=pltpu.CompilerParams(vmem_limit_bytes=48 << 20),
        name="forward_product",
    )(cols, adj, panel)


def backward_product(cols, adj, grad, blocks):
    rows, slots, size, _ = adj.shape
    width = grad.shape[2]
    return pl.pallas_call(
        backward_body,
        out_shape=jax.ShapeDtypeStruct((blocks, width, size), jnp.bfloat16),
        grid_spec=pltpu.PrefetchScalarGridSpec(
            num_scalar_prefetch=1,
            grid=(rows,),
            in_specs=[
                pl.BlockSpec((1, slots, size, size), lambda i, c: (i, 0, 0, 0)),
                pl.BlockSpec((1, size, width), lambda i, c: (i, 0, 0)),
            ],
            out_specs=pl.BlockSpec((blocks, width, size), lambda i, c: (0, 0, 0)),
            scratch_shapes=[pltpu.VMEM((blocks + 1, width, size), jnp.float32)],
        ),
        compiler_params=pltpu.CompilerParams(vmem_limit_bytes=48 << 20),
        name="backward_product",
    )(cols, adj, grad)


def local(features, adjacency, block_cols, block_live, weight, bias, upstream):
    rows, _, slots, size, _ = adjacency.shape
    width = features.shape[1]
    adj = adjacency.reshape(rows, slots, size, size)
    blocks = features.shape[0] * lax.axis_size("row") // size
    live = lax.broadcasted_iota(jnp.int32, (rows, slots), 1) < block_live.reshape(rows)[:, None]
    cols = jnp.where(live, block_cols.reshape(rows, slots), blocks).reshape(-1)
    panel = lax.all_gather(features, "row", axis=0, tiled=True).reshape(blocks, size, width)
    partial = forward_product(cols, adj, panel).reshape(rows * size, width)
    aggregated = lax.psum_scatter(partial, "col", scatter_dimension=0, tiled=True)
    preact = jnp.dot(aggregated, weight, preferred_element_type=jnp.float32) + bias
    s = jax.nn.sigmoid(preact)
    activations = (preact * s).astype(jnp.bfloat16)
    derivative = s * (1.0 + preact * (1.0 - s))
    grad_pre = (upstream.astype(jnp.float32) * derivative).astype(jnp.bfloat16)
    weight_part = jnp.einsum("nf,ng->fg", aggregated, grad_pre, preferred_element_type=jnp.float32)
    bias_part = jnp.sum(grad_pre.astype(jnp.float32), axis=0)
    grad_agg = jnp.einsum("ng,fg->nf", grad_pre, weight, preferred_element_type=jnp.float32).astype(
        jnp.bfloat16
    )
    weight_grad, bias_grad = lax.psum((weight_part, bias_part), ("row", "col"))
    grad = lax.all_gather(grad_agg, "col", axis=0, tiled=True).reshape(rows, size, width)
    turned = backward_product(cols, adj, grad, blocks)
    mine = lax.psum_scatter(turned, "row", scatter_dimension=0, tiled=True)
    feature_grad = mine.transpose(0, 2, 1).reshape(features.shape)
    return (activations, feature_grad, weight_grad, bias_grad)


def solution(mesh):
    placed = (
        P(("col", "row"), None),
        P("row", "col", None, None, None),
        P("row", "col", None),
        P("row", "col"),
        P(),
        P(),
        P(("row", "col"), None),
    )
    return jax.shard_map(
        local,
        mesh=mesh,
        in_specs=placed,
        out_specs=(P(("row", "col"), None), P(("col", "row"), None), P(), P()),
        check_vma=False,
    )
```

```python
import functools

import jax
import jax.numpy as jnp
from jax import lax
from jax.experimental import pallas as pl
from jax.experimental.pallas import tpu as pltpu
from jax.sharding import PartitionSpec as P

MESH = pl.DeviceIdType.MESH
BF16, F32 = jnp.bfloat16, jnp.float32
RING = 4


def dot(a, b, dims=((1,), (0,))):
    return lax.dot_general(a, b, (dims, ((), ())), preferred_element_type=F32)


class Place:
    def __init__(self):
        row, col = lax.axis_index("row"), lax.axis_index("col")
        self.row, self.col = row, col
        self.z, self.x = row // RING, row % RING
        self.y, self.core = col // 2, col % 2

    def rows(self, dz, dx):
        return ((self.z + dz) % RING) * RING + (self.x + dx) % RING

    def cols(self, dy, other=0):
        core = 1 - self.core if other else self.core
        return ((self.y + dy) % RING) * 2 + core

    def plane(self, dz, dx):
        return (self.rows(dz, dx), self.col)

    def line(self, dy, other=0):
        return (self.row, self.cols(dy, other))


class Mail:
    def __init__(self, here, sent, came):
        self.here, self.sent, self.came, self.out = here, sent, came, []

    def make(self, number, src, dst, to):
        return pltpu.make_async_remote_copy(
            src_ref=src, dst_ref=dst, send_sem=self.sent.at[number], recv_sem=self.came.at[number],
            device_id=to, device_id_type=MESH,
        )

    def post(self, number, src, dst, to):
        copy = self.make(number, src, dst, to)
        copy.start()
        self.out.append(copy)

    def take(self, number, dst):
        self.make(number, dst, dst, (self.here.row, self.here.col)).wait_recv()

    def drain(self):
        for copy in self.out:
            copy.wait_send()


def meet(peers):
    barrier = pltpu.get_barrier_semaphore()
    for peer in peers:
        pl.semaphore_signal(barrier, inc=1, device_id=peer, device_id_type=MESH)
    pl.semaphore_wait(barrier, len(peers))


OFFSETS = (0, -1, 1, 2)


def flavour(f, dp, dq):
    return (dq, dp) if f == 0 else (dp, dq)


def gather_rows(mail, base, here, panel):
    def index(f, dp, dq):
        return here.rows(*flavour(f, dp, dq)) * 4 + 2 * f

    def number(f, slot, kind):
        return base + f * 20 + slot * 4 + kind

    def to(f, slot, d):
        return here.plane(*(flavour(f, d, 0) if slot == 0 else flavour(f, 0, d)))

    def pair(f, slot, dp):
        blocks = panel.at[pl.ds(index(f, dp, 0), 2)]
        mail.post(number(f, slot, 0), blocks, blocks, to(f, slot, 1))
        mail.post(number(f, slot, 1), blocks, blocks, to(f, slot, -1))

    def where(f, slot, d):
        return index(f, d, 0) if slot == 0 else index(f, OFFSETS[slot - 1], d)

    def onward(f, slot):
        at = where(f, slot, -1)
        mail.take(number(f, slot, 0), panel.at[pl.ds(at, 2)])
        block = panel.at[pl.ds(at, 1)]
        mail.post(number(f, slot, 2), block, block, to(f, slot, 1))
        at = where(f, slot, 1)
        mail.take(number(f, slot, 1), panel.at[pl.ds(at, 2)])
        block = panel.at[pl.ds(at + 1, 1)]
        mail.post(number(f, slot, 3), block, block, to(f, slot, -1))

    def last(f, slot):
        at = where(f, slot, 2)
        mail.take(number(f, slot, 2), panel.at[pl.ds(at, 1)])
        mail.take(number(f, slot, 3), panel.at[pl.ds(at + 1, 1)])

    both = (0, 1)
    for f in both:
        pair(f, 0, 0)
    for f in both:
        pair(f, 1, 0)
    for f in both:
        onward(f, 0)
        pair(f, 2, -1)
        pair(f, 3, 1)
    for f in both:
        onward(f, 1)
    for f in both:
        last(f, 0)
        pair(f, 4, 2)
    for slot in (2, 3, 4):
        for f in both:
            onward(f, slot)
    for slot in (1, 2, 3, 4):
        for f in both:
            last(f, slot)


GATHER_MAIL = 40
FORWARD_MAIL = GATHER_MAIL + 4 + 6 + 6 + 4


def forward_body(
    cols_ref, live_ref, features_ref, adj_hbm, weight_ref, bias_ref, upstream_ref,
    act_ref, grad_hbm, wpart_ref, bpart_ref,
    panel, adj, cross_out, cross_in, own, line_out, line_in, grads,
    sent, came, adj_sem, out_sem,
):
    here = Place()
    mail = Mail(here, sent, came)
    rows, slots, size, _ = adj.shape
    width = features_ref.shape[1]
    blocks = panel.shape[0] - 1
    piece = features_ref.shape[0]
    half = piece // 2
    per = piece // size
    parts = adj_sem.shape[0]
    step = rows // parts
    fetch = [
        pltpu.make_async_copy(adj_hbm.at[pl.ds(n * step, step)], adj.at[pl.ds(n * step, step)], adj_sem.at[n])
        for n in range(parts)
    ]
    meet([here.plane(0, 1), here.plane(0, -1), here.plane(1, 0), here.plane(-1, 0),
          here.line(1), here.line(-1), here.line(0, 1)])
    for b in range(per):
        panel[here.row * per + b] = features_ref[pl.ds(b * size, size), :]
    panel[blocks] = jnp.zeros_like(panel[blocks])
    for copy in fetch:
        copy.start()
    gather_rows(mail, 0, here, panel)
    for copy in fetch:
        copy.wait()

    def row_product(i):
        total = None
        for k in range(0, slots, 2):
            left = jnp.concatenate([adj[i, k], adj[i, k + 1]], axis=1)
            right = jnp.concatenate(
                [panel[jnp.where(s < live_ref[0, i], cols_ref[s, i], blocks)] for s in (k, k + 1)], axis=0
            )
            part = dot(left, right)
            total = part if total is None else total + part
        return total

    def piece_product(dest, store):
        @pl.loop(0, per)
        def _(n):
            store(pl.ds(pl.multiple_of(n * size, size), size), row_product(dest * per + n))

    order = (2, 1, -1, 0)
    number = GATHER_MAIL
    for n, dy in enumerate(order):
        def store(at, value, n=n):
            cross_out[n, at, :] = value.astype(BF16)

        piece_product(here.cols(dy, 1), store)
        mail.post(number + n, cross_out.at[n], cross_in.at[n], here.line(0, 1))
    for n, dy in enumerate(order):
        def store(at, value, n=n):
            own[n, at, :] = value

        piece_product(here.cols(dy), store)
    low, high = pl.ds(0, half), pl.ds(half, half)

    def chip(n, part):
        return own[n, part, :] + cross_in[n, part, :].astype(F32)

    line = number + 4
    up, down = here.line(1), here.line(-1)
    mail.take(number, cross_in.at[0])
    line_out[0] = chip(0, pl.ds(0, piece)).astype(BF16)
    mail.post(line, line_out.at[0, low], line_in.at[0], up)
    mail.post(line + 1, line_out.at[0, high], line_in.at[1], down)
    mail.take(number + 1, cross_in.at[1])
    line_out[1, high, :] = chip(1, high).astype(BF16)
    mail.post(line + 2, line_out.at[1, high], line_in.at[2], up)
    mail.take(number + 2, cross_in.at[2])
    line_out[2, low, :] = chip(2, low).astype(BF16)
    mail.post(line + 3, line_out.at[2, low], line_in.at[3], down)
    mail.take(line, line_in.at[0])
    line_out[1, low, :] = (chip(1, low) + line_in[0].astype(F32)).astype(BF16)
    mail.post(line + 4, line_out.at[1, low], line_in.at[4], up)
    mail.take(line + 1, line_in.at[1])
    line_out[2, high, :] = (chip(2, high) + line_in[1].astype(F32)).astype(BF16)
    mail.post(line + 5, line_out.at[2, high], line_in.at[5], down)
    mail.take(number + 3, cross_in.at[3])

    ring = line + 6
    across = ring + 6
    mine = here.cols(0)
    wpart = None
    bpart = None
    for part, (a, b) in enumerate(((4, 3), (2, 5))):
        at = low if part == 0 else high
        mail.take(line + a, line_in.at[a])
        mail.take(line + b, line_in.at[b])
        aggregated = (chip(3, at) + line_in[a].astype(F32) + line_in[b].astype(F32)).astype(BF16)
        preact = dot(aggregated, weight_ref[...]) + bias_ref[...]
        s = jax.nn.sigmoid(preact)
        act_ref[at, :] = (preact * s).astype(BF16)
        derivative = s * (1.0 + preact * (1.0 - s))
        grad_pre = (upstream_ref[at, :].astype(F32) * derivative).astype(BF16)
        grads[mine, at, :] = dot(grad_pre, weight_ref[...], ((1,), (1,))).astype(BF16)
        block = grads.at[mine, at]
        mail.post(ring + 2 * part, block, block, up)
        mail.post(ring + 2 * part + 1, block, block, down)
        w = dot(aggregated, grad_pre, ((0,), (0,)))
        b8 = jnp.sum(grad_pre.astype(F32).reshape(half // 8, 8, width), axis=0)
        wpart = w if wpart is None else wpart + w
        bpart = b8 if bpart is None else bpart + b8
    mail.post(across, grads.at[mine], grads.at[mine], here.line(0, 1))
    wpart_ref[...] = wpart
    bpart_ref[...] = bpart

    def out(c, n):
        copy = pltpu.make_async_copy(grads.at[c], grad_hbm.at[c], out_sem.at[n])
        copy.start()
        return copy

    copies = [out(mine, 0)]
    before, after, far = here.cols(-1), here.cols(1), here.cols(2)
    mail.take(ring, grads.at[before, low])
    block = grads.at[before, low]
    mail.post(ring + 4, block, block, up)
    mail.take(ring + 1, grads.at[after, low])
    mail.take(ring + 3, grads.at[after, high])
    block = grads.at[after, high]
    mail.post(ring + 5, block, block, down)
    mail.post(across + 1, grads.at[after], grads.at[after], here.line(0, 1))
    copies.append(out(after, 1))
    mail.take(ring + 2, grads.at[before, high])
    mail.post(across + 2, grads.at[before], grads.at[before], here.line(0, 1))
    copies.append(out(before, 2))
    mail.take(ring + 4, grads.at[far, low])
    mail.take(ring + 5, grads.at[far, high])
    mail.post(across + 3, grads.at[far], grads.at[far], here.line(0, 1))
    copies.append(out(far, 3))
    for n, dy in enumerate((0, 1, -1, 2)):
        c = here.cols(dy, 1)
        mail.take(across + n, grads.at[c])
        copies.append(out(c, 4 + n))
    for copy in copies:
        copy.wait()
    mail.drain()


def forward_layer(cols, live, features, adj, weight, bias, upstream):
    rows, slots, size, _ = adj.shape
    piece, width = features.shape
    blocks = lax.axis_size("row") * piece // size
    pieces = lax.axis_size("col")
    vmem, anywhere = pl.BlockSpec(memory_space=pltpu.VMEM), pl.BlockSpec(memory_space=pl.ANY)
    smem = pl.BlockSpec(memory_space=pltpu.SMEM)
    return pl.pallas_call(
        forward_body,
        out_shape=(
            jax.ShapeDtypeStruct((piece, width), BF16),
            jax.ShapeDtypeStruct((pieces, piece, width), BF16),
            jax.ShapeDtypeStruct((width, width), F32),
            jax.ShapeDtypeStruct((8, width), F32),
        ),
        in_specs=[smem, smem, vmem, anywhere, vmem, vmem, vmem],
        out_specs=(vmem, anywhere, vmem, vmem),
        scratch_shapes=[
            pltpu.VMEM((blocks + 1, size, width), BF16),
            pltpu.VMEM(adj.shape, BF16),
            pltpu.VMEM((4, piece, width), BF16),
            pltpu.VMEM((4, piece, width), BF16),
            pltpu.VMEM((4, piece, width), F32),
            pltpu.VMEM((3, piece, width), BF16),
            pltpu.VMEM((6, piece // 2, width), BF16),
            pltpu.VMEM((pieces, piece, width), BF16),
            pltpu.SemaphoreType.DMA((FORWARD_MAIL,)),
            pltpu.SemaphoreType.DMA((FORWARD_MAIL,)),
            pltpu.SemaphoreType.DMA((4,)),
            pltpu.SemaphoreType.DMA((8,)),
        ],
        compiler_params=pltpu.CompilerParams(
            collective_id=0, has_side_effects=True, vmem_limit_bytes=56 << 20
        ),
        name="forward_layer",
    )(cols, live, features, adj, weight, bias, upstream)


def backward_body(cols_ref, live_ref, adj_ref, grad_ref, out_ref, acc_ref):
    i = pl.program_id(0)
    slots, size = adj_ref.shape[1], adj_ref.shape[3]
    blocks = out_ref.shape[0]

    @pl.when(i == 0)
    def _():
        acc_ref[...] = jnp.zeros_like(acc_ref)

    turned = grad_ref[0].T
    for k in range(0, slots, 2):
        right = jnp.concatenate([adj_ref[0, k], adj_ref[0, k + 1]], axis=1)
        part = dot(turned, right)
        for s in (0, 1):
            j = jnp.where(k + s < live_ref[0, i], cols_ref[k + s, i], blocks)
            acc_ref[j] += part[:, s * size : (s + 1) * size]

    @pl.when(i == pl.num_programs(0) - 1)
    def _():
        @pl.loop(0, out_ref.shape[0])
        def _(j):
            out_ref[j] = acc_ref[j].astype(out_ref.dtype)


def backward_product(cols, live, adj, grad, blocks):
    rows, slots, size, _ = adj.shape
    width = grad.shape[2]
    return pl.pallas_call(
        backward_body,
        out_shape=jax.ShapeDtypeStruct((blocks, width, size), BF16),
        grid_spec=pltpu.PrefetchScalarGridSpec(
            num_scalar_prefetch=2,
            grid=(rows,),
            in_specs=[
                pl.BlockSpec((1, slots, size, size), lambda i, c, l: (i, 0, 0, 0)),
                pl.BlockSpec((1, size, width), lambda i, c, l: (i, 0, 0)),
            ],
            out_specs=pl.BlockSpec((blocks, width, size), lambda i, c, l: (0, 0, 0)),
            scratch_shapes=[pltpu.VMEM((blocks + 1, width, size), F32)],
        ),
        compiler_params=pltpu.CompilerParams(vmem_limit_bytes=48 << 20),
        name="backward_product",
    )(cols, live, adj, grad)


SCATTER_MAIL = 60
LINE_MAIL, SLICE_MAIL = 7, 3
BACK_MAIL = SCATTER_MAIL + 2 * LINE_MAIL + 3 * SLICE_MAIL


def back_body(
    turned_ref, wpart_ref, bpart_ref, feature_grad_ref, wgrad_ref, bgrad_ref,
    rx, tx, stage, w_out, w_in, x_out, x_in, z_in, slab, sent, came,
):
    here = Place()
    mail = Mail(here, sent, came)
    size = turned_ref.shape[2]
    nx = w_out.shape[0]
    slice_rows = wpart_ref.shape[0] // nx
    thin = slice_rows // RING
    peers = [here.plane(0, 1), here.plane(0, -1), here.plane(0, 2), here.plane(1, 0), here.plane(-1, 0), here.plane(2, 0)]
    peers += [(here.row, (here.col + d) % nx) for d in range(1, nx)]
    meet(peers)

    for d in range(1, nx):
        c = (here.col + d) % nx
        w_out[c, :slice_rows] = wpart_ref[pl.ds(c * slice_rows, slice_rows), :]
        w_out[c, slice_rows:] = bpart_ref[...]
    w_in[here.col, :slice_rows] = wpart_ref[pl.ds(here.col * slice_rows, slice_rows), :]
    w_in[here.col, slice_rows:] = bpart_ref[...]
    base = SCATTER_MAIL
    for d in range(1, nx):
        c = (here.col + d) % nx
        mail.post(base + d - 1, w_out.at[c], w_in.at[here.col], (here.row, c))

    def number(f, slot, kind):
        return f * 30 + slot * 6 + kind

    def to(f, slot, d):
        return here.plane(*(flavour(f, d, 0) if slot < 4 else flavour(f, 0, d)))

    def source(f, slot, d, b):
        if slot < 4:
            return turned_ref.at[here.rows(*flavour(f, d, OFFSETS[slot])) * 4 + 2 * f + b]
        return stage.at[f, OFFSETS.index(d), b]

    def send(f, slot, kind, d, b):
        n = number(f, slot, kind)
        if slot < 4:
            src = source(f, slot, 2 if kind < 2 else d, b)
        else:
            src = tx.at[n]
            tx[n] = source(f, slot, 2 if kind < 2 else d, b)[...].astype(BF16)
        mail.post(n, src, rx.at[n], to(f, slot, d))

    def first(f, slot):
        send(f, slot, 0, 1, 0)
        send(f, slot, 1, -1, 1)

    def direct(f, slot):
        send(f, slot, 2, 1, 1)
        send(f, slot, 3, -1, 0)

    def onward(f, slot):
        for kind, d, b in ((0, 1, 0), (1, -1, 1)):
            mail.take(number(f, slot, kind), rx.at[number(f, slot, kind)])
            n = number(f, slot, 4 + kind)
            tx[n] = (source(f, slot, d, b)[...].astype(F32) + rx[number(f, slot, kind)].astype(F32)).astype(BF16)
            mail.post(n, tx.at[n], rx.at[n], to(f, slot, d))

    def total(f, slot, b):
        result = source(f, slot, 0, b)[...].astype(F32)
        for kind in ((4, 3) if b == 0 else (2, 5)):
            n = number(f, slot, kind)
            mail.take(n, rx.at[n])
            result = result + rx[n].astype(F32)
        return result

    both = (0, 1)
    order = (3, 1, 2, 0)
    for slot in order:
        for f in both:
            first(f, slot)
    for slot in order:
        for f in both:
            direct(f, slot)

    def finish(slot):
        for f in both:
            for b in (0, 1):
                stage[f, slot, b] = total(f, slot, b)

    for f in both:
        onward(f, 3)
    for d in range(1, nx):
        mail.take(base + d - 1, w_in.at[(here.col + nx - d) % nx])
    got = w_in[0]
    for c in range(1, nx):
        got = got + w_in[c]
    second = base + nx - 1
    for n in range(RING):
        x_out[n, :thin] = got[n * thin : (n + 1) * thin]
        x_out[n, thin:] = got[slice_rows:]
    x_in[here.x] = x_out[here.x]
    for d in range(1, RING):
        x = (here.x + d) % RING
        mail.post(second + d - 1, x_out.at[x], x_in.at[here.x], here.plane(0, d))
    for f in both:
        onward(f, 1)
        onward(f, 2)
    finish(3)
    for f in both:
        first(f, 4)
    for f in both:
        onward(f, 0)
    for d in range(1, RING):
        mail.take(second + d - 1, x_in.at[(here.x + RING - d) % RING])
    got = x_in[0]
    for n in range(1, RING):
        got = got + x_in[n]
    z_in[here.z] = got
    third = second + SLICE_MAIL
    for d in range(1, RING):
        mail.post(third + d - 1, z_in.at[here.z], z_in.at[here.z], here.plane(d, 0))
    finish(1)
    finish(2)
    for f in both:
        direct(f, 4)
    for f in both:
        onward(f, 4)
    for d in range(1, RING):
        mail.take(third + d - 1, z_in.at[(here.z + RING - d) % RING])
    got = z_in[0]
    for n in range(1, RING):
        got = got + z_in[n]
    bgrad_ref[...] = jnp.sum(got[thin:], axis=0, keepdims=True)
    slab[here.x] = got[:thin]
    fourth = third + SLICE_MAIL
    for d in range(1, RING):
        mail.post(fourth + d - 1, slab.at[here.x], slab.at[here.x], here.plane(0, d))
    finish(0)
    for d in range(1, RING):
        mail.take(fourth + d - 1, slab.at[(here.x + RING - d) % RING])
    fifth = fourth + SLICE_MAIL
    w_out[here.col, :slice_rows] = slab[...].reshape(slice_rows, slab.shape[2])
    wgrad_ref[pl.ds(here.col * slice_rows, slice_rows), :] = w_out[here.col, :slice_rows]
    for d in range(1, nx):
        part = wgrad_ref.at[pl.ds(here.col * slice_rows, slice_rows)]
        mail.post(fifth + d - 1, part, part, (here.row, (here.col + d) % nx))
    for f in both:
        for b in (0, 1):
            feature_grad_ref[pl.ds((2 * f + b) * size, size), :] = total(f, 4, b).T.astype(BF16)
    for d in range(1, nx):
        c = (here.col + nx - d) % nx
        mail.take(fifth + d - 1, wgrad_ref.at[pl.ds(c * slice_rows, slice_rows)])
    mail.drain()


def back_sums(turned, wpart, bpart, piece):
    _, width, size = turned.shape
    nx = lax.axis_size("col")
    slice_rows = width // nx
    vmem = pl.BlockSpec(memory_space=pltpu.VMEM)
    return pl.pallas_call(
        back_body,
        out_shape=(
            jax.ShapeDtypeStruct((piece, width), BF16),
            jax.ShapeDtypeStruct((width, width), F32),
            jax.ShapeDtypeStruct((1, width), F32),
        ),
        in_specs=[vmem, vmem, vmem],
        out_specs=(vmem, vmem, vmem),
        scratch_shapes=[
            pltpu.VMEM((60, width, size), BF16),
            pltpu.VMEM((60, width, size), BF16),
            pltpu.VMEM((2, 4, 2, width, size), F32),
            pltpu.VMEM((nx, slice_rows + 8, width), F32),
            pltpu.VMEM((nx, slice_rows + 8, width), F32),
            pltpu.VMEM((RING, slice_rows // RING + 8, width), F32),
            pltpu.VMEM((RING, slice_rows // RING + 8, width), F32),
            pltpu.VMEM((RING, slice_rows // RING + 8, width), F32),
            pltpu.VMEM((RING, slice_rows // RING, width), F32),
            pltpu.SemaphoreType.DMA((BACK_MAIL,)),
            pltpu.SemaphoreType.DMA((BACK_MAIL,)),
        ],
        compiler_params=pltpu.CompilerParams(
            collective_id=1, has_side_effects=True, vmem_limit_bytes=48 << 20
        ),
        name="back_sums",
    )(turned, wpart, bpart)


def local(features, adjacency, block_cols, block_live, weight, bias, upstream):
    rows, _, slots, size, _ = adjacency.shape
    piece, width = features.shape
    adj = adjacency.reshape(rows, slots, size, size)
    blocks = piece * lax.axis_size("row") // size
    cols = block_cols.reshape(rows, slots).T
    live = block_live.reshape(1, rows)
    act, grads, wpart, bpart = forward_layer(
        cols, live, features, adj, weight, bias.reshape(1, width), upstream
    )
    turned = backward_product(cols, live, adj, grads.reshape(rows, size, width), blocks)
    feature_grad, wgrad, bgrad = back_sums(turned, wpart, bpart, piece)
    return act, feature_grad, wgrad, bgrad.reshape(width)


def solution(mesh):
    placed = (
        P(("col", "row"), None),
        P("row", "col", None, None, None),
        P("row", "col", None),
        P("row", "col"),
        P(),
        P(),
        P(("row", "col"), None),
    )
    return jax.shard_map(
        local,
        mesh=mesh,
        in_specs=placed,
        out_specs=(P(("row", "col"), None), P(("col", "row"), None), P(), P()),
        check_vma=False,
    )
```

```python
import functools

import jax
import jax.numpy as jnp
from jax import lax
from jax.experimental import pallas as pl
from jax.experimental.pallas import tpu as pltpu
from jax.sharding import PartitionSpec as P

MESH = pl.DeviceIdType.MESH
BF16, F32 = jnp.bfloat16, jnp.float32
RING = 4


def dot(a, b, dims=((1,), (0,))):
    return lax.dot_general(a, b, (dims, ((), ())), preferred_element_type=F32)


class Place:
    def __init__(self):
        row, col = lax.axis_index("row"), lax.axis_index("col")
        self.row, self.col = row, col
        self.z, self.x = row // RING, row % RING
        self.y, self.core = col // 2, col % 2

    def rows(self, dz, dx):
        return ((self.z + dz) % RING) * RING + (self.x + dx) % RING

    def cols(self, dy, other=0):
        core = 1 - self.core if other else self.core
        return ((self.y + dy) % RING) * 2 + core

    def plane(self, dz, dx):
        return (self.rows(dz, dx), self.col)

    def line(self, dy, other=0):
        return (self.row, self.cols(dy, other))


class Mail:
    def __init__(self, here, sent, came):
        self.here, self.sent, self.came, self.out = here, sent, came, []

    def make(self, number, src, dst, to):
        return pltpu.make_async_remote_copy(
            src_ref=src, dst_ref=dst, send_sem=self.sent.at[number], recv_sem=self.came.at[number],
            device_id=to, device_id_type=MESH,
        )

    def post(self, number, src, dst, to):
        copy = self.make(number, src, dst, to)
        copy.start()
        self.out.append(copy)

    def take(self, number, dst):
        self.make(number, dst, dst, (self.here.row, self.here.col)).wait_recv()

    def drain(self):
        for copy in self.out:
            copy.wait_send()


def meet(peers):
    barrier = pltpu.get_barrier_semaphore()
    for peer in peers:
        pl.semaphore_signal(barrier, inc=1, device_id=peer, device_id_type=MESH)
    pl.semaphore_wait(barrier, len(peers))


OFFSETS = (0, -1, 1, 2)


def flavour(f, dp, dq):
    return (dq, dp) if f == 0 else (dp, dq)


def gather_rows(mail, base, here, panel):
    def index(f, dp, dq):
        return here.rows(*flavour(f, dp, dq)) * 4 + 2 * f

    def number(f, slot, kind):
        return base + f * 20 + slot * 4 + kind

    def to(f, slot, d):
        return here.plane(*(flavour(f, d, 0) if slot == 0 else flavour(f, 0, d)))

    def pair(f, slot, dp):
        blocks = panel.at[pl.ds(index(f, dp, 0), 2)]
        mail.post(number(f, slot, 0), blocks, blocks, to(f, slot, 1))
        mail.post(number(f, slot, 1), blocks, blocks, to(f, slot, -1))

    def where(f, slot, d):
        return index(f, d, 0) if slot == 0 else index(f, OFFSETS[slot - 1], d)

    def onward(f, slot):
        at = where(f, slot, -1)
        mail.take(number(f, slot, 0), panel.at[pl.ds(at, 2)])
        block = panel.at[pl.ds(at, 1)]
        mail.post(number(f, slot, 2), block, block, to(f, slot, 1))
        at = where(f, slot, 1)
        mail.take(number(f, slot, 1), panel.at[pl.ds(at, 2)])
        block = panel.at[pl.ds(at + 1, 1)]
        mail.post(number(f, slot, 3), block, block, to(f, slot, -1))

    def last(f, slot):
        at = where(f, slot, 2)
        mail.take(number(f, slot, 2), panel.at[pl.ds(at, 1)])
        mail.take(number(f, slot, 3), panel.at[pl.ds(at + 1, 1)])

    both = (0, 1)
    for f in both:
        pair(f, 0, 0)
    for f in both:
        pair(f, 1, 0)
    for f in both:
        onward(f, 0)
        pair(f, 2, -1)
        pair(f, 3, 1)
    for f in both:
        onward(f, 1)
    for f in both:
        last(f, 0)
        pair(f, 4, 2)
    for slot in (2, 3, 4):
        for f in both:
            onward(f, slot)
    for slot in (1, 2, 3, 4):
        for f in both:
            last(f, slot)


GATHER_MAIL = 40
FORWARD_MAIL = GATHER_MAIL + 4 + 6 + 6 + 5
EXTRA = 8


def forward_body(
    cols_ref, live_ref, features_ref, adj_hbm, weight_ref, bias_ref, upstream_ref,
    act_ref, grad_hbm, wpart_ref, bpart_ref,
    panel, adj, cross_out, cross_in, own, line_out, line_in, grads,
    sent, came, adj_sem, out_sem,
):
    here = Place()
    mail = Mail(here, sent, came)
    rows, slots, size, _ = adj.shape
    width = features_ref.shape[1]
    blocks = panel.shape[0] - 1
    piece = features_ref.shape[0]
    half = piece // 2
    per = piece // size
    parts = adj_sem.shape[0]
    step = rows // parts
    fetch = [
        pltpu.make_async_copy(adj_hbm.at[pl.ds(n * step, step)], adj.at[pl.ds(n * step, step)], adj_sem.at[n])
        for n in range(parts)
    ]
    meet([here.plane(0, 1), here.plane(0, -1), here.plane(1, 0), here.plane(-1, 0),
          here.line(1), here.line(-1), here.line(0, 1)])
    for b in range(per):
        panel[here.row * per + b] = features_ref[pl.ds(b * size, size), :]
    panel[blocks] = jnp.zeros_like(panel[blocks])
    for copy in fetch:
        copy.start()
    gather_rows(mail, 0, here, panel)
    for copy in fetch:
        copy.wait()

    def row_product(i):
        total = None
        for k in range(0, slots, 2):
            left = jnp.concatenate([adj[i, k], adj[i, k + 1]], axis=1)
            right = jnp.concatenate(
                [panel[jnp.where(s < live_ref[0, i], cols_ref[s, 0, i], blocks)] for s in (k, k + 1)], axis=0
            )
            part = dot(left, right)
            total = part if total is None else total + part
        return total

    def piece_product(dest, out):
        for n in range(per):
            out[n * size : (n + 1) * size, :] = row_product(dest * per + n).astype(out.dtype)

    number = GATHER_MAIL
    offsets = (2, 1, -1, 0)

    def cross(n):
        piece_product(here.cols(offsets[n], 1), cross_out.at[n])
        mail.post(number + n, cross_out.at[n], cross_in.at[n], here.line(0, 1))

    def keep(n):
        piece_product(here.cols(offsets[n]), own.at[n])
        mail.take(number + n, cross_in.at[n])

    low, high = pl.ds(0, half), pl.ds(half, half)

    def chip(n, part):
        return own[n, part, :] + cross_in[n, part, :].astype(F32)

    line = number + 4
    up, down = here.line(1), here.line(-1)
    cross(0)
    cross(1)
    keep(0)
    line_out[0] = chip(0, pl.ds(0, piece)).astype(BF16)
    mail.post(line, line_out.at[0, low], line_in.at[0], up)
    mail.post(line + 1, line_out.at[0, high], line_in.at[1], down)
    cross(2)
    keep(1)
    line_out[1, high, :] = chip(1, high).astype(BF16)
    mail.post(line + 2, line_out.at[1, high], line_in.at[2], up)
    cross(3)
    keep(2)
    line_out[2, low, :] = chip(2, low).astype(BF16)
    mail.post(line + 3, line_out.at[2, low], line_in.at[3], down)
    mail.take(line, line_in.at[0])
    line_out[1, low, :] = (chip(1, low) + line_in[0].astype(F32)).astype(BF16)
    mail.post(line + 4, line_out.at[1, low], line_in.at[4], up)
    mail.take(line + 1, line_in.at[1])
    line_out[2, high, :] = (chip(2, high) + line_in[1].astype(F32)).astype(BF16)
    mail.post(line + 5, line_out.at[2, high], line_in.at[5], down)
    keep(3)

    ring = line + 6
    across = ring + 6
    mine = here.cols(0)
    wpart = None
    bpart = None
    for part, (a, b) in enumerate(((4, 3), (2, 5))):
        at = low if part == 0 else high
        mail.take(line + a, line_in.at[a])
        mail.take(line + b, line_in.at[b])
        aggregated = (chip(3, at) + line_in[a].astype(F32) + line_in[b].astype(F32)).astype(BF16)
        preact = dot(aggregated, weight_ref[...]) + bias_ref[...]
        s = jax.nn.sigmoid(preact)
        act_ref[at, :] = (preact * s).astype(BF16)
        derivative = s * (1.0 + preact * (1.0 - s))
        grad_pre = (upstream_ref[at, :].astype(F32) * derivative).astype(BF16)
        grads[mine, at, :] = dot(grad_pre, weight_ref[...], ((1,), (1,))).astype(BF16)
        block = grads.at[mine, at]
        mail.post(ring + 2 * part, block, block, up)
        mail.post(ring + 2 * part + 1, block, block, down)
        w = dot(aggregated, grad_pre, ((0,), (0,)))
        b8 = jnp.sum(grad_pre.astype(F32).reshape(half // 8, 8, width), axis=0)
        wpart = w if wpart is None else wpart + w
        bpart = b8 if bpart is None else bpart + b8
    mail.post(across, grads.at[mine], grads.at[mine], here.line(0, 1))
    wpart_ref[...] = wpart
    bpart_ref[...] = bpart

    def out(c, n):
        copy = pltpu.make_async_copy(grads.at[c], grad_hbm.at[c], out_sem.at[n])
        copy.start()
        return copy

    copies = [out(mine, 0)]
    before, after, far = here.cols(-1), here.cols(1), here.cols(2)
    mail.take(ring, grads.at[before, low])
    block = grads.at[before, low]
    mail.post(ring + 4, block, block, up)
    mail.take(ring + 1, grads.at[after, low])
    mail.take(ring + 3, grads.at[after, high])
    block = grads.at[after, high]
    mail.post(ring + 5, block, block, down)
    mail.post(across + 1, grads.at[after], grads.at[after], here.line(0, 1))
    copies.append(out(after, 1))
    mail.take(ring + 2, grads.at[before, high])
    mail.post(across + 2, grads.at[before], grads.at[before], here.line(0, 1))
    copies.append(out(before, 2))
    for n, at in enumerate((low, high)):
        mail.take(ring + 4 + n, grads.at[far, at])
        mail.post(across + 3 + n, grads.at[far, at], grads.at[far, at], here.line(0, 1))
    copies.append(out(far, 3))
    for n, dy in enumerate((0, 1, -1, 2)):
        c = here.cols(dy, 1)
        if n < 3:
            mail.take(across + n, grads.at[c])
        else:
            mail.take(across + 3, grads.at[c, low])
            mail.take(across + 4, grads.at[c, high])
        copies.append(out(c, 4 + n))
    for copy in copies:
        copy.wait()
    mail.drain()


def forward_layer(cols, live, features, adj, weight, bias, upstream):
    rows, slots, size, _ = adj.shape
    piece, width = features.shape
    blocks = lax.axis_size("row") * piece // size
    pieces = lax.axis_size("col")
    vmem, anywhere = pl.BlockSpec(memory_space=pltpu.VMEM), pl.BlockSpec(memory_space=pl.ANY)
    smem = pl.BlockSpec(memory_space=pltpu.SMEM)
    return pl.pallas_call(
        forward_body,
        out_shape=(
            jax.ShapeDtypeStruct((piece, width), BF16),
            jax.ShapeDtypeStruct((pieces, piece, width), BF16),
            jax.ShapeDtypeStruct((width, width), F32),
            jax.ShapeDtypeStruct((8, width), F32),
        ),
        in_specs=[smem, smem, vmem, anywhere, vmem, vmem, vmem],
        out_specs=(vmem, anywhere, vmem, vmem),
        scratch_shapes=[
            pltpu.VMEM((blocks + 1, size, width), BF16),
            pltpu.VMEM(adj.shape, BF16),
            pltpu.VMEM((4, piece, width), BF16),
            pltpu.VMEM((4, piece, width), BF16),
            pltpu.VMEM((4, piece, width), F32),
            pltpu.VMEM((3, piece, width), BF16),
            pltpu.VMEM((6, piece // 2, width), BF16),
            pltpu.VMEM((pieces, piece, width), BF16),
            pltpu.SemaphoreType.DMA((FORWARD_MAIL,)),
            pltpu.SemaphoreType.DMA((FORWARD_MAIL,)),
            pltpu.SemaphoreType.DMA((4,)),
            pltpu.SemaphoreType.DMA((8,)),
        ],
        compiler_params=pltpu.CompilerParams(
            collective_id=0, has_side_effects=True, vmem_limit_bytes=56 << 20
        ),
        name="forward_layer",
    )(cols, live, features, adj, weight, bias, upstream)


PARTS = 4


def backward_body(
    cols_ref, live_ref, adj_hbm, grad_hbm, act_hbm, out, act_out_hbm, adj, grad, acc, in_sem, act_sem
):
    rows, slots, size, _ = adj.shape
    blocks = out.shape[0]
    step, group = rows // PARTS, blocks // PARTS

    def fetch(n):
        at = pl.ds(n * step, step)
        return (
            pltpu.make_async_copy(adj_hbm.at[at], adj.at[at], in_sem.at[0, n]),
            pltpu.make_async_copy(grad_hbm.at[at], grad.at[at], in_sem.at[1, n]),
        )

    for n in range(PARTS):
        for copy in fetch(n):
            copy.start()
    passing = pltpu.make_async_copy(act_hbm, act_out_hbm, act_sem)
    passing.start()

    @pl.loop(0, blocks)
    def _(j):
        acc[j] = jnp.zeros_like(acc[j])

    @pl.loop(0, PARTS)
    def _(n):
        for copy in fetch(n):
            copy.wait()
        for u in range(step):
            i = n * step + u
            for k in range(slots):
                j = jnp.where(k < live_ref[0, i], cols_ref[k, 0, i], blocks)
                acc[j] += dot(adj[i, k], grad[i], ((0,), (0,)))

    @pl.loop(0, PARTS)
    def _(n):
        for u in range(group):
            out[n * group + u] = acc[n * group + u].astype(out.dtype)

    passing.wait()


def backward_product(cols, live, adj, grad, act, blocks):
    rows, slots, size, _ = adj.shape
    width = grad.shape[2]
    vmem, smem, anywhere = pl.BlockSpec(memory_space=pltpu.VMEM), pl.BlockSpec(memory_space=pltpu.SMEM), pl.BlockSpec(memory_space=pl.ANY)
    return pl.pallas_call(
        backward_body,
        out_shape=(
            jax.ShapeDtypeStruct((blocks, size, width), BF16),
            jax.ShapeDtypeStruct(act.shape, BF16),
        ),
        in_specs=[smem, smem, anywhere, anywhere, anywhere],
        out_specs=(vmem, anywhere),
        scratch_shapes=[
            pltpu.VMEM(adj.shape, BF16),
            pltpu.VMEM(grad.shape, BF16),
            pltpu.VMEM((blocks + 1, size, width), F32),
            pltpu.SemaphoreType.DMA((2, PARTS)),
            pltpu.SemaphoreType.DMA,
        ],
        compiler_params=pltpu.CompilerParams(vmem_limit_bytes=40 << 20),
        name="backward_product",
    )(cols, live, adj, grad, act)


SCATTER_MAIL = 60
LINE_MAIL, SLICE_MAIL = 7, 3
BACK_MAIL = SCATTER_MAIL + 2 * LINE_MAIL + 3 * SLICE_MAIL


def back_body(
    sums_ref, wpart_ref, bpart_ref, feature_grad_ref, wgrad_ref, bgrad_ref,
    rx, tx, stage, w_out, w_in, x_out, x_in, z_in, slab, sent, came,
):
    here = Place()
    mail = Mail(here, sent, came)
    size = sums_ref.shape[1]
    nx = w_out.shape[0]
    slice_rows = wpart_ref.shape[0] // nx
    thin = slice_rows // RING
    peers = [here.plane(*at) for at in ((0, 1), (0, -1), (0, 2), (1, 0), (-1, 0), (2, 0))]
    peers += [(here.row, (here.col + d) % nx) for d in range(1, nx)]
    for d in range(1, nx):
        c = (here.col + d) % nx
        w_out[c, :slice_rows] = wpart_ref[pl.ds(c * slice_rows, slice_rows), :]
        w_out[c, slice_rows:] = bpart_ref[...]
    w_in[here.col, :slice_rows] = wpart_ref[pl.ds(here.col * slice_rows, slice_rows), :]
    w_in[here.col, slice_rows:] = bpart_ref[...]
    meet(peers)
    base = SCATTER_MAIL
    for d in range(1, nx):
        c = (here.col + d) % nx
        mail.post(base + d - 1, w_out.at[c], w_in.at[here.col], (here.row, c))

    def number(f, slot, kind):
        return f * 30 + slot * 6 + kind

    def to(f, slot, d):
        return here.plane(*(flavour(f, d, 0) if slot < 4 else flavour(f, 0, d)))

    def source(f, slot, d, b):
        if slot < 4:
            return sums_ref.at[here.rows(*flavour(f, d, OFFSETS[slot])) * 4 + 2 * f + b]
        return stage.at[f, OFFSETS.index(d), b]

    def send(f, slot, kind, d, b):
        n = number(f, slot, kind)
        if slot < 4:
            src = source(f, slot, 2 if kind < 2 else d, b)
        else:
            src = tx.at[n]
            tx[n] = source(f, slot, 2 if kind < 2 else d, b)[...].astype(BF16)
        mail.post(n, src, rx.at[n], to(f, slot, d))

    def first(f, slot):
        send(f, slot, 0, 1, 0)
        send(f, slot, 1, -1, 1)

    def direct(f, slot):
        send(f, slot, 2, 1, 1)
        send(f, slot, 3, -1, 0)

    def onward(f, slot):
        for kind, d, b in ((0, 1, 0), (1, -1, 1)):
            mail.take(number(f, slot, kind), rx.at[number(f, slot, kind)])
            n = number(f, slot, 4 + kind)
            tx[n] = (source(f, slot, d, b)[...].astype(F32) + rx[number(f, slot, kind)].astype(F32)).astype(BF16)
            mail.post(n, tx.at[n], rx.at[n], to(f, slot, d))

    def total(f, slot, b):
        result = source(f, slot, 0, b)[...].astype(F32)
        for kind in ((4, 3) if b == 0 else (2, 5)):
            n = number(f, slot, kind)
            mail.take(n, rx.at[n])
            result = result + rx[n].astype(F32)
        return result

    both = (0, 1)

    def finish(slot):
        for f in both:
            for b in (0, 1):
                stage[f, slot, b] = total(f, slot, b)

    second = base + nx - 1
    third = second + SLICE_MAIL
    fourth = third + SLICE_MAIL
    fifth = fourth + SLICE_MAIL

    def added(parts, count):
        got = parts[0]
        for n in range(1, count):
            got = got + parts[n]
        return got

    def column_sums():
        for d in range(1, nx):
            mail.take(base + d - 1, w_in.at[(here.col + nx - d) % nx])
        got = added(w_in, nx)
        for n in range(RING):
            x_out[n, :thin] = got[n * thin : (n + 1) * thin]
            x_out[n, thin:] = got[slice_rows:]
        x_in[here.x] = x_out[here.x]
        for d in range(1, RING):
            mail.post(second + d - 1, x_out.at[(here.x + d) % RING], x_in.at[here.x], here.plane(0, d))

    def x_sums():
        for d in range(1, RING):
            mail.take(second + d - 1, x_in.at[(here.x + RING - d) % RING])
        z_in[here.z] = added(x_in, RING)
        for d in range(1, RING):
            mail.post(third + d - 1, z_in.at[here.z], z_in.at[here.z], here.plane(d, 0))

    def z_sums():
        for d in range(1, RING):
            mail.take(third + d - 1, z_in.at[(here.z + RING - d) % RING])
        got = added(z_in, RING)
        bgrad_ref[...] = jnp.sum(got[thin:], axis=0, keepdims=True)
        slab[here.x] = got[:thin]
        for d in range(1, RING):
            mail.post(fourth + d - 1, slab.at[here.x], slab.at[here.x], here.plane(0, d))

    mine = pl.ds(here.col * slice_rows, slice_rows)

    def spread():
        for d in range(1, RING):
            mail.take(fourth + d - 1, slab.at[(here.x + RING - d) % RING])
        for n in range(RING):
            wgrad_ref[pl.ds(here.col * slice_rows + n * thin, thin), :] = slab[n]
        for d in range(1, nx):
            mail.post(fifth + d - 1, wgrad_ref.at[mine], wgrad_ref.at[mine], (here.row, (here.col + d) % nx))

    def each(action, *slots):
        for slot in slots:
            for f in both:
                action(f, slot)

    each(first, 3)
    each(direct, 3)
    each(first, 1)
    each(onward, 3)
    each(first, 2)
    column_sums()
    each(onward, 1)
    each(direct, 1)
    x_sums()
    each(onward, 2)
    each(direct, 2)
    finish(3)
    each(first, 4)
    each(first, 0)
    z_sums()
    each(direct, 0)
    finish(1)
    finish(2)
    each(onward, 4)
    each(direct, 4)
    spread()
    each(onward, 0)
    finish(0)
    for f in both:
        for b in (0, 1):
            feature_grad_ref[pl.ds((2 * f + b) * size, size), :] = total(f, 4, b).astype(BF16)
    for d in range(1, nx):
        c = (here.col + nx - d) % nx
        mail.take(fifth + d - 1, wgrad_ref.at[pl.ds(c * slice_rows, slice_rows)])
    mail.drain()


def back_sums(sums, wpart, bpart, piece):
    _, size, width = sums.shape
    nx = lax.axis_size("col")
    slice_rows = width // nx
    vmem = pl.BlockSpec(memory_space=pltpu.VMEM)
    return pl.pallas_call(
        back_body,
        out_shape=(
            jax.ShapeDtypeStruct((piece, width), BF16),
            jax.ShapeDtypeStruct((width, width), F32),
            jax.ShapeDtypeStruct((1, width), F32),
        ),
        in_specs=[vmem, vmem, vmem],
        out_specs=(vmem, vmem, vmem),
        scratch_shapes=[
            pltpu.VMEM((SCATTER_MAIL, size, width), BF16),
            pltpu.VMEM((SCATTER_MAIL, size, width), BF16),
            pltpu.VMEM((2, 4, 2, size, width), F32),
            pltpu.VMEM((nx, slice_rows + EXTRA, width), F32),
            pltpu.VMEM((nx, slice_rows + EXTRA, width), F32),
            pltpu.VMEM((RING, slice_rows // RING + EXTRA, width), F32),
            pltpu.VMEM((RING, slice_rows // RING + EXTRA, width), F32),
            pltpu.VMEM((RING, slice_rows // RING + EXTRA, width), F32),
            pltpu.VMEM((RING, slice_rows // RING, width), F32),
            pltpu.SemaphoreType.DMA((BACK_MAIL,)),
            pltpu.SemaphoreType.DMA((BACK_MAIL,)),
        ],
        compiler_params=pltpu.CompilerParams(
            collective_id=1, has_side_effects=True, vmem_limit_bytes=24 << 20
        ),
        name="back_sums",
    )(sums, wpart, bpart)


def hand_over(*arrays):
    def body(*refs):
        for source, target in zip(refs[: len(arrays)], refs[len(arrays) :]):
            target[...] = source[...]

    vmem = pl.BlockSpec(memory_space=pltpu.VMEM)
    return pl.pallas_call(
        body,
        out_shape=tuple(jax.ShapeDtypeStruct(a.shape, a.dtype) for a in arrays),
        in_specs=[vmem] * len(arrays),
        out_specs=(vmem,) * len(arrays),
        compiler_params=pltpu.CompilerParams(vmem_limit_bytes=4 << 20),
        name="hand_over",
    )(*arrays)


def local(features, adjacency, block_cols, block_live, weight, bias, upstream):
    rows, _, slots, size, _ = adjacency.shape
    piece, width = features.shape
    adj = adjacency.reshape(rows, slots, size, size)
    blocks = piece * lax.axis_size("row") // size
    cols = block_cols.transpose(2, 1, 0)
    live = block_live.reshape(1, rows)
    act, grads, wpart, bpart = forward_layer(
        cols, live, features, adj, weight, bias.reshape(1, width), upstream
    )
    sums, act = backward_product(cols, live, adj, grads.reshape(rows, size, width), act, blocks)
    feature_grad, wgrad, bgrad = hand_over(*back_sums(sums, wpart, bpart, piece))
    return act, feature_grad, wgrad, bgrad.reshape(width)


def solution(mesh):
    placed = (
        P(("col", "row"), None),
        P("row", "col", None, None, None),
        P("row", "col", None),
        P("row", "col"),
        P(),
        P(),
        P(("row", "col"), None),
    )
    return jax.shard_map(
        local,
        mesh=mesh,
        in_specs=placed,
        out_specs=(P(("row", "col"), None), P(("col", "row"), None), P(), P()),
        check_vma=False,
    )
```

```python
import functools

import jax
import jax.numpy as jnp
from jax import lax
from jax.experimental import pallas as pl
from jax.experimental.pallas import tpu as pltpu
from jax.sharding import PartitionSpec as P

MESH = pl.DeviceIdType.MESH
BF16, F32 = jnp.bfloat16, jnp.float32
RING = 4


def dot(a, b, dims=((1,), (0,))):
    return lax.dot_general(a, b, (dims, ((), ())), preferred_element_type=F32)


class Place:
    def __init__(self):
        row, col = lax.axis_index("row"), lax.axis_index("col")
        self.row, self.col = row, col
        self.z, self.x = row // RING, row % RING
        self.y, self.core = col // 2, col % 2

    def rows(self, dz, dx):
        return ((self.z + dz) % RING) * RING + (self.x + dx) % RING

    def cols(self, dy, other=0):
        core = 1 - self.core if other else self.core
        return ((self.y + dy) % RING) * 2 + core

    def plane(self, dz, dx):
        return (self.rows(dz, dx), self.col)

    def line(self, dy, other=0):
        return (self.row, self.cols(dy, other))


class Mail:
    def __init__(self, here, sent, came):
        self.here, self.sent, self.came, self.out = here, sent, came, []

    def make(self, number, src, dst, to):
        return pltpu.make_async_remote_copy(
            src_ref=src, dst_ref=dst, send_sem=self.sent.at[number], recv_sem=self.came.at[number],
            device_id=to, device_id_type=MESH,
        )

    def post(self, number, src, dst, to):
        copy = self.make(number, src, dst, to)
        copy.start()
        self.out.append(copy)

    def take(self, number, dst):
        self.make(number, dst, dst, (self.here.row, self.here.col)).wait_recv()

    def drain(self):
        for copy in self.out:
            copy.wait_send()


def greet(peers):
    barrier = pltpu.get_barrier_semaphore()
    for peer in peers:
        pl.semaphore_signal(barrier, inc=1, device_id=peer, device_id_type=MESH)
    return barrier, len(peers)


def meet(peers):
    pl.semaphore_wait(*greet(peers))


OFFSETS = (0, -1, 1, 2)


def flavour(f, dp, dq):
    return (dq, dp) if f == 0 else (dp, dq)


def gather_rows(mail, base, here, panel):
    def view(at, count):
        return panel.at[pl.ds(at, count)]

    def index(f, dp, dq):
        return here.rows(*flavour(f, dp, dq)) * 4 + 2 * f

    def number(f, slot, kind):
        return base + f * 20 + slot * 4 + kind

    def to(f, slot, d):
        return here.plane(*(flavour(f, d, 0) if slot == 0 else flavour(f, 0, d)))

    def pair(f, slot, dp):
        blocks = view(index(f, dp, 0), 2)
        mail.post(number(f, slot, 0), blocks, blocks, to(f, slot, 1))
        mail.post(number(f, slot, 1), blocks, blocks, to(f, slot, -1))

    def where(f, slot, d):
        return index(f, d, 0) if slot == 0 else index(f, OFFSETS[slot - 1], d)

    def onward(f, slot):
        at = where(f, slot, -1)
        mail.take(number(f, slot, 0), view(at, 2))
        mail.post(number(f, slot, 2), view(at, 1), view(at, 1), to(f, slot, 1))
        at = where(f, slot, 1)
        mail.take(number(f, slot, 1), view(at, 2))
        mail.post(number(f, slot, 3), view(at + 1, 1), view(at + 1, 1), to(f, slot, -1))

    def last(f, slot):
        at = where(f, slot, 2)
        mail.take(number(f, slot, 2), view(at, 1))
        mail.take(number(f, slot, 3), view(at + 1, 1))

    both = (0, 1)
    for slot in (0, 1):
        for f in both:
            pair(f, slot, 0)
    for f in both:
        onward(f, 0)
        pair(f, 2, -1)
        pair(f, 3, 1)
    for f in both:
        onward(f, 1)
    for f in both:
        last(f, 0)
        pair(f, 4, 2)
    for slot in (2, 3, 4):
        for f in both:
            onward(f, slot)
    for slot in (1, 2, 3, 4):
        for f in both:
            last(f, slot)


GATHER_MAIL = 40
FORWARD_MAIL = GATHER_MAIL + 4 + 6 + 6 + 5
EXTRA = 8


def forward_body(
    cols_ref, live_ref, features_hbm, adj_hbm, weight_hbm, bias_hbm, upstream_hbm,
    act_ref, grad_hbm, wpart_ref, bpart_ref,
    panel, adj, weight, bias, upstream, cross_out, cross_in, own, line_out, line_in, grads,
    sent, came, adj_sem, out_sem, in_sem,
):
    here = Place()
    mail = Mail(here, sent, came)
    rows, slots, size, _ = adj.shape
    per, _, width = features_hbm.shape
    blocks = panel.shape[0] - 1
    piece = per * size
    parts = adj_sem.shape[0]
    step = rows // parts
    mine = pltpu.make_async_copy(features_hbm, panel.at[pl.ds(here.row * per, per)], in_sem.at[0])
    later = [
        pltpu.make_async_copy(source, target, in_sem.at[1 + n])
        for n, (source, target) in enumerate(((weight_hbm, weight), (bias_hbm, bias), (upstream_hbm, upstream)))
    ]
    later += [
        pltpu.make_async_copy(adj_hbm.at[pl.ds(n * step, step)], adj.at[pl.ds(n * step, step)], adj_sem.at[n])
        for n in range(parts)
    ]
    barrier = greet([here.plane(0, 1), here.plane(0, -1), here.plane(1, 0), here.plane(-1, 0),
                     here.line(1), here.line(-1), here.line(0, 1)])
    for copy in [mine] + later:
        copy.start()
    panel[blocks] = jnp.zeros_like(panel[blocks])
    mine.wait()
    pl.semaphore_wait(*barrier)
    gather_rows(mail, 0, here, panel)
    for copy in later:
        copy.wait()

    half = piece // 2

    def row_product(i):
        left = jnp.concatenate([adj[i, k] for k in range(slots)], axis=1)
        right = jnp.concatenate(
            [panel[jnp.where(k < live_ref[0, i], cols_ref[k, 0, i], blocks)] for k in range(slots)], axis=0
        )
        return dot(left, right)

    def piece_product(dest, out):
        for n in range(per):
            out[n * size : (n + 1) * size, :] = row_product(dest * per + n).astype(out.dtype)

    number = GATHER_MAIL
    offsets = (2, 1, -1, 0)

    def cross(n):
        piece_product(here.cols(offsets[n], 1), cross_out.at[n])
        mail.post(number + n, cross_out.at[n], cross_in.at[n], here.line(0, 1))

    def keep(n):
        piece_product(here.cols(offsets[n]), own.at[n])
        mail.take(number + n, cross_in.at[n])

    low, high = pl.ds(0, half), pl.ds(half, half)

    def chip(n, part):
        return own[n, part, :] + cross_in[n, part, :].astype(F32)

    line = number + 4
    up, down = here.line(1), here.line(-1)
    cross(0)
    keep(0)
    line_out[0] = chip(0, pl.ds(0, piece)).astype(BF16)
    mail.post(line, line_out.at[0, low], line_in.at[0], up)
    mail.post(line + 1, line_out.at[0, high], line_in.at[1], down)
    cross(1)
    keep(1)
    line_out[1, high, :] = chip(1, high).astype(BF16)
    mail.post(line + 2, line_out.at[1, high], line_in.at[2], up)
    cross(2)
    keep(2)
    line_out[2, low, :] = chip(2, low).astype(BF16)
    mail.post(line + 3, line_out.at[2, low], line_in.at[3], down)
    mail.take(line, line_in.at[0])
    line_out[1, low, :] = (chip(1, low) + line_in[0].astype(F32)).astype(BF16)
    mail.post(line + 4, line_out.at[1, low], line_in.at[4], up)
    mail.take(line + 1, line_in.at[1])
    line_out[2, high, :] = (chip(2, high) + line_in[1].astype(F32)).astype(BF16)
    mail.post(line + 5, line_out.at[2, high], line_in.at[5], down)
    cross(3)
    keep(3)

    ring = line + 6
    across = ring + 6
    mine = here.cols(0)
    wpart = None
    bpart = None
    for part, (a, b) in enumerate(((4, 3), (2, 5))):
        at = low if part == 0 else high
        mail.take(line + a, line_in.at[a])
        mail.take(line + b, line_in.at[b])
        aggregated = (chip(3, at) + line_in[a].astype(F32) + line_in[b].astype(F32)).astype(BF16)
        preact = dot(aggregated, weight[...]) + bias[...]
        s = jax.nn.sigmoid(preact)
        act_ref[at, :] = (preact * s).astype(BF16)
        derivative = s * (1.0 + preact * (1.0 - s))
        grad_pre = (upstream[at, :].astype(F32) * derivative).astype(BF16)
        grads[mine, at, :] = dot(grad_pre, weight[...], ((1,), (1,))).astype(BF16)
        block = grads.at[mine, at]
        mail.post(ring + 2 * part, block, block, up)
        mail.post(ring + 2 * part + 1, block, block, down)
        w = dot(aggregated, grad_pre, ((0,), (0,)))
        b8 = jnp.sum(grad_pre.astype(F32).reshape(half // 8, 8, width), axis=0)
        wpart = w if wpart is None else wpart + w
        bpart = b8 if bpart is None else bpart + b8
    mail.post(across, grads.at[mine], grads.at[mine], here.line(0, 1))
    wpart_ref[...] = wpart
    bpart_ref[...] = bpart

    def out(c, n):
        copy = pltpu.make_async_copy(grads.at[c], grad_hbm.at[c], out_sem.at[n])
        copy.start()
        return copy

    copies = [out(mine, 0)]
    before, after, far = here.cols(-1), here.cols(1), here.cols(2)
    mail.take(ring, grads.at[before, low])
    block = grads.at[before, low]
    mail.post(ring + 4, block, block, up)
    mail.take(ring + 1, grads.at[after, low])
    mail.take(ring + 3, grads.at[after, high])
    block = grads.at[after, high]
    mail.post(ring + 5, block, block, down)
    mail.post(across + 1, grads.at[after], grads.at[after], here.line(0, 1))
    copies.append(out(after, 1))
    mail.take(ring + 2, grads.at[before, high])
    mail.post(across + 2, grads.at[before], grads.at[before], here.line(0, 1))
    copies.append(out(before, 2))
    for n, at in enumerate((low, high)):
        mail.take(ring + 4 + n, grads.at[far, at])
        mail.post(across + 3 + n, grads.at[far, at], grads.at[far, at], here.line(0, 1))
    copies.append(out(far, 3))
    for n, dy in enumerate((0, 1, -1, 2)):
        c = here.cols(dy, 1)
        if n < 3:
            mail.take(across + n, grads.at[c])
        else:
            mail.take(across + 3, grads.at[c, low])
            mail.take(across + 4, grads.at[c, high])
        copies.append(out(c, 4 + n))
    for copy in copies:
        copy.wait()
    mail.drain()


def forward_layer(cols, live, features, adj, weight, bias, upstream):
    rows, slots, size, _ = adj.shape
    per, _, width = features.shape
    piece = per * size
    blocks = lax.axis_size("row") * piece // size
    pieces = lax.axis_size("col")
    vmem, anywhere = pl.BlockSpec(memory_space=pltpu.VMEM), pl.BlockSpec(memory_space=pl.ANY)
    smem = pl.BlockSpec(memory_space=pltpu.SMEM)
    return pl.pallas_call(
        forward_body,
        out_shape=(
            jax.ShapeDtypeStruct((piece, width), BF16),
            jax.ShapeDtypeStruct((SPACE * pieces, piece, width), BF16),
            jax.ShapeDtypeStruct((width, width), F32),
            jax.ShapeDtypeStruct((8, width), F32),
        ),
        in_specs=[smem, smem] + [anywhere] * 5,
        out_specs=(vmem, anywhere, vmem, vmem),
        scratch_shapes=[
            pltpu.VMEM((blocks + 1, size, width), BF16),
            pltpu.VMEM(adj.shape, BF16),
            pltpu.VMEM(weight.shape, BF16),
            pltpu.VMEM(bias.shape, F32),
            pltpu.VMEM(upstream.shape, BF16),
            pltpu.VMEM((4, piece, width), BF16),
            pltpu.VMEM((4, piece, width), BF16),
            pltpu.VMEM((4, piece, width), F32),
            pltpu.VMEM((3, piece, width), BF16),
            pltpu.VMEM((6, piece // 2, width), BF16),
            pltpu.VMEM((pieces, piece, width), BF16),
            pltpu.SemaphoreType.DMA((FORWARD_MAIL,)),
            pltpu.SemaphoreType.DMA((FORWARD_MAIL,)),
            pltpu.SemaphoreType.DMA((4,)),
            pltpu.SemaphoreType.DMA((8,)),
            pltpu.SemaphoreType.DMA((4,)),
        ],
        compiler_params=pltpu.CompilerParams(
            collective_id=0, has_side_effects=True, vmem_limit_bytes=56 << 20
        ),
        name="forward_layer",
    )(cols, live, features, adj, weight, bias, upstream)


PARTS = 4
SPACE = 16


def backward_body(
    cols_ref, live_ref, adj_hbm, grad_hbm, out, adj, grad, acc, in_sem
):
    rows, slots, size, _ = adj.shape
    blocks = out.shape[0]
    step, group = rows // PARTS, blocks // PARTS

    def fetch(n):
        at = pl.ds(n * step, step)
        return (
            pltpu.make_async_copy(adj_hbm.at[at], adj.at[at], in_sem.at[0, n]),
            pltpu.make_async_copy(grad_hbm.at[at], grad.at[at], in_sem.at[1, n]),
        )

    for n in range(PARTS):
        for copy in fetch(n):
            copy.start()

    @pl.loop(0, blocks)
    def _(j):
        acc[j] = jnp.zeros_like(acc[j])

    @pl.loop(0, PARTS)
    def _(n):
        for copy in fetch(n):
            copy.wait()
        for u in range(step):
            i = n * step + u
            for k in range(slots):
                j = jnp.where(k < live_ref[0, i], cols_ref[k, 0, i], blocks)
                acc[j] += dot(adj[i, k], grad[i], ((0,), (0,)))

    @pl.loop(0, PARTS)
    def _(n):
        for u in range(group):
            out[n * group + u] = acc[n * group + u].astype(out.dtype)


def backward_product(cols, live, adj, grad, blocks):
    rows, slots, size, _ = adj.shape
    width = grad.shape[2]
    vmem, smem, anywhere = pl.BlockSpec(memory_space=pltpu.VMEM), pl.BlockSpec(memory_space=pltpu.SMEM), pl.BlockSpec(memory_space=pl.ANY)
    return pl.pallas_call(
        backward_body,
        out_shape=jax.ShapeDtypeStruct((blocks, size, width), BF16),
        in_specs=[smem, smem, anywhere, anywhere],
        out_specs=vmem,
        scratch_shapes=[
            pltpu.VMEM(adj.shape, BF16),
            pltpu.VMEM((rows, size, width), BF16),
            pltpu.VMEM((blocks + 1, size, width), F32),
            pltpu.SemaphoreType.DMA((2, PARTS)),
        ],
        compiler_params=pltpu.CompilerParams(vmem_limit_bytes=40 << 20),
        name="backward_product",
    )(cols, live, adj, grad)


SCATTER_MAIL = 60
LINE_MAIL, SLICE_MAIL = 7, 3
BACK_MAIL = SCATTER_MAIL + 2 * LINE_MAIL + 3 * SLICE_MAIL


def back_body(
    sums_ref, wpart_ref, bpart_ref, feature_grad_ref, wgrad_ref, bgrad_ref,
    rx, tx, stage, w_out, w_in, x_out, x_in, z_in, slab, sent, came,
):
    here = Place()
    mail = Mail(here, sent, came)
    size = sums_ref.shape[1]
    nx = w_out.shape[0]
    slice_rows = wpart_ref.shape[0] // nx
    thin = slice_rows // RING
    peers = [here.plane(*at) for at in ((0, 1), (0, -1), (0, 2), (1, 0), (-1, 0), (2, 0))]
    peers += [(here.row, (here.col + d) % nx) for d in range(1, nx)]
    for d in range(1, nx):
        c = (here.col + d) % nx
        w_out[c, :slice_rows] = wpart_ref[pl.ds(c * slice_rows, slice_rows), :]
        w_out[c, slice_rows:] = bpart_ref[...]
    w_in[here.col, :slice_rows] = wpart_ref[pl.ds(here.col * slice_rows, slice_rows), :]
    w_in[here.col, slice_rows:] = bpart_ref[...]
    meet(peers)
    base = SCATTER_MAIL
    for d in range(1, nx):
        c = (here.col + d) % nx
        mail.post(base + d - 1, w_out.at[c], w_in.at[here.col], (here.row, c))

    def number(f, slot, kind):
        return f * 30 + slot * 6 + kind

    def to(f, slot, d):
        return here.plane(*(flavour(f, d, 0) if slot < 4 else flavour(f, 0, d)))

    def source(f, slot, d, b):
        if slot < 4:
            return sums_ref.at[here.rows(*flavour(f, d, OFFSETS[slot])) * 4 + 2 * f + b]
        return stage.at[f, OFFSETS.index(d), b]

    def send(f, slot, kind, d, b):
        n = number(f, slot, kind)
        if slot < 4:
            src = source(f, slot, 2 if kind < 2 else d, b)
        else:
            src = tx.at[n]
            tx[n] = source(f, slot, 2 if kind < 2 else d, b)[...].astype(BF16)
        mail.post(n, src, rx.at[n], to(f, slot, d))

    def first(f, slot):
        send(f, slot, 0, 1, 0)
        send(f, slot, 1, -1, 1)

    def direct(f, slot):
        send(f, slot, 2, 1, 1)
        send(f, slot, 3, -1, 0)

    def onward(f, slot):
        for kind, d, b in ((0, 1, 0), (1, -1, 1)):
            mail.take(number(f, slot, kind), rx.at[number(f, slot, kind)])
            n = number(f, slot, 4 + kind)
            tx[n] = (source(f, slot, d, b)[...].astype(F32) + rx[number(f, slot, kind)].astype(F32)).astype(BF16)
            mail.post(n, tx.at[n], rx.at[n], to(f, slot, d))

    def total(f, slot, b):
        result = source(f, slot, 0, b)[...].astype(F32)
        for kind in ((4, 3) if b == 0 else (2, 5)):
            n = number(f, slot, kind)
            mail.take(n, rx.at[n])
            result = result + rx[n].astype(F32)
        return result

    both = (0, 1)

    def finish(slot):
        for f in both:
            for b in (0, 1):
                stage[f, slot, b] = total(f, slot, b)

    second = base + nx - 1
    third = second + SLICE_MAIL
    fourth = third + SLICE_MAIL
    fifth = fourth + SLICE_MAIL

    def added(parts, count):
        got = parts[0]
        for n in range(1, count):
            got = got + parts[n]
        return got

    def column_sums():
        for d in range(1, nx):
            mail.take(base + d - 1, w_in.at[(here.col + nx - d) % nx])
        got = added(w_in, nx)
        for n in range(RING):
            x_out[n, :thin] = got[n * thin : (n + 1) * thin]
            x_out[n, thin:] = got[slice_rows:]
        x_in[here.x] = x_out[here.x]
        for d in range(1, RING):
            mail.post(second + d - 1, x_out.at[(here.x + d) % RING], x_in.at[here.x], here.plane(0, d))

    def x_sums():
        for d in range(1, RING):
            mail.take(second + d - 1, x_in.at[(here.x + RING - d) % RING])
        z_in[here.z] = added(x_in, RING)
        for d in range(1, RING):
            mail.post(third + d - 1, z_in.at[here.z], z_in.at[here.z], here.plane(d, 0))

    def z_sums():
        for d in range(1, RING):
            mail.take(third + d - 1, z_in.at[(here.z + RING - d) % RING])
        got = added(z_in, RING)
        bgrad_ref[...] = jnp.sum(got[thin:], axis=0, keepdims=True)
        slab[here.x] = got[:thin]
        for d in range(1, RING):
            mail.post(fourth + d - 1, slab.at[here.x], slab.at[here.x], here.plane(0, d))

    mine = pl.ds(here.col * slice_rows, slice_rows)

    def spread():
        for d in range(1, RING):
            mail.take(fourth + d - 1, slab.at[(here.x + RING - d) % RING])
        for n in range(RING):
            wgrad_ref[pl.ds(here.col * slice_rows + n * thin, thin), :] = slab[n]
        for d in range(1, nx):
            mail.post(fifth + d - 1, wgrad_ref.at[mine], wgrad_ref.at[mine], (here.row, (here.col + d) % nx))

    def each(action, *slots):
        for slot in slots:
            for f in both:
                action(f, slot)

    each(first, 3)
    each(direct, 3)
    each(first, 1)
    each(onward, 3)
    each(first, 2)
    column_sums()
    each(onward, 1)
    each(direct, 1)
    x_sums()
    each(onward, 2)
    each(direct, 2)
    finish(3)
    each(first, 4)
    each(first, 0)
    z_sums()
    each(direct, 0)
    finish(1)
    finish(2)
    each(onward, 4)
    each(direct, 4)
    spread()
    each(onward, 0)
    finish(0)
    for f in both:
        for b in (0, 1):
            feature_grad_ref[pl.ds((2 * f + b) * size, size), :] = total(f, 4, b).astype(BF16)
    for d in range(1, nx):
        c = (here.col + nx - d) % nx
        mail.take(fifth + d - 1, wgrad_ref.at[pl.ds(c * slice_rows, slice_rows)])
    mail.drain()


def back_sums(sums, wpart, bpart, piece):
    _, size, width = sums.shape
    nx = lax.axis_size("col")
    slice_rows = width // nx
    vmem = pl.BlockSpec(memory_space=pltpu.VMEM)
    return pl.pallas_call(
        back_body,
        out_shape=(
            jax.ShapeDtypeStruct((piece, width), BF16),
            jax.ShapeDtypeStruct((width, width), F32),
            jax.ShapeDtypeStruct((1, width), F32),
        ),
        in_specs=[vmem, vmem, vmem],
        out_specs=(vmem, vmem, vmem),
        scratch_shapes=[
            pltpu.VMEM((SCATTER_MAIL, size, width), BF16),
            pltpu.VMEM((SCATTER_MAIL, size, width), BF16),
            pltpu.VMEM((2, 4, 2, size, width), F32),
            pltpu.VMEM((nx, slice_rows + EXTRA, width), F32),
            pltpu.VMEM((nx, slice_rows + EXTRA, width), F32),
            pltpu.VMEM((RING, slice_rows // RING + EXTRA, width), F32),
            pltpu.VMEM((RING, slice_rows // RING + EXTRA, width), F32),
            pltpu.VMEM((RING, slice_rows // RING + EXTRA, width), F32),
            pltpu.VMEM((RING, slice_rows // RING, width), F32),
            pltpu.SemaphoreType.DMA((BACK_MAIL,)),
            pltpu.SemaphoreType.DMA((BACK_MAIL,)),
        ],
        compiler_params=pltpu.CompilerParams(
            collective_id=1, has_side_effects=True, vmem_limit_bytes=24 << 20
        ),
        name="back_sums",
    )(sums, wpart, bpart)


def hand_over(*arrays):
    def body(*refs):
        for source, target in zip(refs[: len(arrays)], refs[len(arrays) :]):
            target[...] = source[...]

    vmem = pl.BlockSpec(memory_space=pltpu.VMEM)
    return pl.pallas_call(
        body,
        out_shape=tuple(jax.ShapeDtypeStruct(a.shape, a.dtype) for a in arrays),
        in_specs=[vmem] * len(arrays),
        out_specs=(vmem,) * len(arrays),
        compiler_params=pltpu.CompilerParams(vmem_limit_bytes=4 << 20),
        name="hand_over",
    )(*arrays)


def local(features, adjacency, block_cols, block_live, weight, bias, upstream):
    rows, _, slots, size, _ = adjacency.shape
    piece, width = features.shape
    adj = adjacency.reshape(rows, slots, size, size)
    blocks = piece * lax.axis_size("row") // size
    cols = block_cols.transpose(2, 1, 0)
    live = block_live.reshape(1, rows)
    act, grads, wpart, bpart = forward_layer(
        cols, live, features.reshape(piece // size, size, width), adj, weight, bias.reshape(1, width), upstream
    )
    sums = backward_product(cols, live, adj, grads.reshape(SPACE * rows, size, width), blocks)
    act, feature_grad, wgrad, bgrad = hand_over(act, *back_sums(sums, wpart, bpart, piece))
    return act, feature_grad, wgrad, bgrad.reshape(width)


def solution(mesh):
    placed = (
        P(("col", "row"), None),
        P("row", "col", None, None, None),
        P("row", "col", None),
        P("row", "col"),
        P(),
        P(),
        P(("row", "col"), None),
    )
    return jax.shard_map(
        local,
        mesh=mesh,
        in_specs=placed,
        out_specs=(P(("row", "col"), None), P(("col", "row"), None), P(), P()),
        check_vma=False,
    )
```

```python
import functools

import jax
import jax.numpy as jnp
from jax import lax
from jax.experimental import pallas as pl
from jax.experimental.pallas import tpu as pltpu
from jax.sharding import PartitionSpec as P

MESH = pl.DeviceIdType.MESH
BF16, F32 = jnp.bfloat16, jnp.float32
RING = 4


def dot(a, b, dims=((1,), (0,))):
    return lax.dot_general(a, b, (dims, ((), ())), preferred_element_type=F32)


class Place:
    def __init__(self):
        row, col = lax.axis_index("row"), lax.axis_index("col")
        self.row, self.col = row, col
        self.z, self.x = row // RING, row % RING
        self.y, self.core = col // 2, col % 2

    def rows(self, dz, dx):
        return ((self.z + dz) % RING) * RING + (self.x + dx) % RING

    def cols(self, dy, other=0):
        core = 1 - self.core if other else self.core
        return ((self.y + dy) % RING) * 2 + core

    def plane(self, dz, dx):
        return (self.rows(dz, dx), self.col)

    def line(self, dy, other=0):
        return (self.row, self.cols(dy, other))


class Mail:
    def __init__(self, here, sent, came):
        self.here, self.sent, self.came, self.out = here, sent, came, []

    def make(self, number, src, dst, to):
        return pltpu.make_async_remote_copy(
            src_ref=src, dst_ref=dst, send_sem=self.sent.at[number], recv_sem=self.came.at[number],
            device_id=to, device_id_type=MESH,
        )

    def post(self, number, src, dst, to):
        copy = self.make(number, src, dst, to)
        copy.start()
        self.out.append(copy)

    def take(self, number, dst):
        self.make(number, dst, dst, (self.here.row, self.here.col)).wait_recv()

    def drain(self):
        for copy in self.out:
            copy.wait_send()


def greet(peers):
    barrier = pltpu.get_barrier_semaphore()
    for peer in peers:
        pl.semaphore_signal(barrier, inc=1, device_id=peer, device_id_type=MESH)
    return barrier, len(peers)


OFFSETS = (0, -1, 1, 2)


def flavour(f, dp, dq):
    return (dq, dp) if f == 0 else (dp, dq)


def gather_rows(mail, base, here, panel):
    def view(at, count):
        return panel.at[pl.ds(at, count)]

    def index(f, dp, dq):
        return here.rows(*flavour(f, dp, dq)) * 4 + 2 * f

    def number(f, slot, kind):
        return base + f * 20 + slot * 4 + kind

    def to(f, slot, d):
        return here.plane(*(flavour(f, d, 0) if slot == 0 else flavour(f, 0, d)))

    def pair(f, slot, dp):
        blocks = view(index(f, dp, 0), 2)
        mail.post(number(f, slot, 0), blocks, blocks, to(f, slot, 1))
        mail.post(number(f, slot, 1), blocks, blocks, to(f, slot, -1))

    def where(f, slot, d):
        return index(f, d, 0) if slot == 0 else index(f, OFFSETS[slot - 1], d)

    def onward(f, slot):
        at = where(f, slot, -1)
        mail.take(number(f, slot, 0), view(at, 2))
        mail.post(number(f, slot, 2), view(at, 1), view(at, 1), to(f, slot, 1))
        at = where(f, slot, 1)
        mail.take(number(f, slot, 1), view(at, 2))
        mail.post(number(f, slot, 3), view(at + 1, 1), view(at + 1, 1), to(f, slot, -1))

    def last(f, slot):
        at = where(f, slot, 2)
        mail.take(number(f, slot, 2), view(at, 1))
        mail.take(number(f, slot, 3), view(at + 1, 1))

    both = (0, 1)
    for slot in (0, 1):
        for f in both:
            pair(f, slot, 0)
    for f in both:
        onward(f, 0)
        pair(f, 2, -1)
        pair(f, 3, 1)
    for f in both:
        onward(f, 1)
    for f in both:
        last(f, 0)
        pair(f, 4, 2)
    for slot in (2, 3, 4):
        for f in both:
            onward(f, slot)
    for slot in (1, 2, 3, 4):
        for f in both:
            last(f, slot)


GATHER_MAIL = 40
FORWARD_MAIL = GATHER_MAIL + 4 + 6 + 6 + 5 + 1
EXTRA = 8


def forward_body(
    cols_ref, live_ref, features_hbm, adj_hbm, weight_hbm, bias_hbm, upstream_hbm,
    act_ref, grad_hbm, wpart_ref, bpart_ref,
    panel, adj, weight, bias, upstream, cross_out, cross_in, own, line_out, line_in, grads,
    sent, came, adj_sem, out_sem, in_sem,
):
    here = Place()
    mail = Mail(here, sent, came)
    rows, slots, size, _ = adj.shape
    per, _, width = features_hbm.shape
    blocks = panel.shape[0] - 1
    piece = per * size
    parts = adj_sem.shape[0]
    step = rows // parts
    mine = pltpu.make_async_copy(features_hbm, panel.at[pl.ds(here.row * per, per)], in_sem.at[0])
    later = [
        pltpu.make_async_copy(source, target, in_sem.at[1 + n])
        for n, (source, target) in enumerate(((weight_hbm, weight), (bias_hbm, bias), (upstream_hbm, upstream)))
    ]
    later += [
        pltpu.make_async_copy(adj_hbm.at[pl.ds(n * step, step)], adj.at[pl.ds(n * step, step)], adj_sem.at[n])
        for n in range(parts)
    ]
    barrier = greet([here.plane(0, 1), here.plane(0, -1), here.plane(1, 0), here.plane(-1, 0),
                     here.line(1), here.line(-1), here.line(0, 1)])
    for copy in [mine] + later:
        copy.start()
    panel[blocks] = jnp.zeros_like(panel[blocks])
    mine.wait()
    pl.semaphore_wait(*barrier)
    gather_rows(mail, 0, here, panel)
    for copy in later:
        copy.wait()

    half = piece // 2

    def row_product(i):
        left = jnp.concatenate([adj[i, k] for k in range(slots)], axis=1)
        right = jnp.concatenate(
            [panel[jnp.where(k < live_ref[0, i], cols_ref[k, 0, i], blocks)] for k in range(slots)], axis=0
        )
        return dot(left, right)

    def piece_product(dest, out):
        for n in range(per):
            out[n * size : (n + 1) * size, :] = row_product(dest * per + n).astype(out.dtype)

    number = GATHER_MAIL
    offsets = (2, 1, -1, 0)

    def cross(n):
        piece_product(here.cols(offsets[n], 1), cross_out.at[n])
        mail.post(number + n, cross_out.at[n], cross_in.at[n], here.line(0, 1))

    def keep(n):
        piece_product(here.cols(offsets[n]), own.at[n])
        mail.take(number + n, cross_in.at[n])

    low, high = pl.ds(0, half), pl.ds(half, half)

    def chip(n, part):
        return own[n, part, :] + cross_in[n, part, :].astype(F32)

    line = number + 4
    up, down = here.line(1), here.line(-1)
    halves = (low, high)
    spare = FORWARD_MAIL - 1

    def half_product(dest, part, out):
        for n in range(per // 2):
            rows_at = part.start + n * size
            out[rows_at : rows_at + size, :] = row_product(dest * per + rows_at // size).astype(out.dtype)

    for part, at in zip(halves, (number, spare)):
        half_product(here.cols(offsets[0], 1), part, cross_out.at[0])
        mail.post(at, cross_out.at[0, part], cross_in.at[0, part], here.line(0, 1))
    for n, (part, at, to) in enumerate(zip(halves, (number, spare), (up, down))):
        half_product(here.cols(offsets[0]), part, own.at[0])
        mail.take(at, cross_in.at[0, part])
        line_out[0, part, :] = chip(0, part).astype(BF16)
        mail.post(line + n, line_out.at[0, part], line_in.at[n], to)
    cross(1)
    keep(1)
    line_out[1, high, :] = chip(1, high).astype(BF16)
    mail.post(line + 2, line_out.at[1, high], line_in.at[2], up)
    cross(2)
    keep(2)
    line_out[2, low, :] = chip(2, low).astype(BF16)
    mail.post(line + 3, line_out.at[2, low], line_in.at[3], down)
    mail.take(line, line_in.at[0])
    line_out[1, low, :] = (chip(1, low) + line_in[0].astype(F32)).astype(BF16)
    mail.post(line + 4, line_out.at[1, low], line_in.at[4], up)
    mail.take(line + 1, line_in.at[1])
    line_out[2, high, :] = (chip(2, high) + line_in[1].astype(F32)).astype(BF16)
    mail.post(line + 5, line_out.at[2, high], line_in.at[5], down)
    cross(3)
    keep(3)

    ring = line + 6
    across = ring + 6
    mine = here.cols(0)
    wpart = None
    bpart = None
    for part, (a, b) in enumerate(((4, 3), (2, 5))):
        at = low if part == 0 else high
        mail.take(line + a, line_in.at[a])
        mail.take(line + b, line_in.at[b])
        aggregated = (chip(3, at) + line_in[a].astype(F32) + line_in[b].astype(F32)).astype(BF16)
        preact = dot(aggregated, weight[...]) + bias[...]
        s = jax.nn.sigmoid(preact)
        act_ref[at, :] = (preact * s).astype(BF16)
        derivative = s * (1.0 + preact * (1.0 - s))
        grad_pre = (upstream[at, :].astype(F32) * derivative).astype(BF16)
        grads[mine, at, :] = dot(grad_pre, weight[...], ((1,), (1,))).astype(BF16)
        block = grads.at[mine, at]
        if part == 0:
            mail.post(ring, block, block, up)
        else:
            mail.post(ring + 3, block, block, down)
            mail.post(ring + 2, block, block, up)
            block = grads.at[mine, low]
            mail.post(ring + 1, block, block, down)
        w = dot(aggregated, grad_pre, ((0,), (0,)))
        b8 = jnp.sum(grad_pre.astype(F32).reshape(half // 8, 8, width), axis=0)
        wpart = w if wpart is None else wpart + w
        bpart = b8 if bpart is None else bpart + b8
    mail.post(across, grads.at[mine], grads.at[mine], here.line(0, 1))
    wpart_ref[...] = wpart
    bpart_ref[...] = bpart

    def out(c, n):
        copy = pltpu.make_async_copy(grads.at[c], grad_hbm.at[c], out_sem.at[n])
        copy.start()
        return copy

    copies = [out(mine, 0)]
    before, after, far = here.cols(-1), here.cols(1), here.cols(2)
    mail.take(ring, grads.at[before, low])
    block = grads.at[before, low]
    mail.post(ring + 4, block, block, up)
    mail.take(ring + 3, grads.at[after, high])
    block = grads.at[after, high]
    mail.post(ring + 5, block, block, down)
    mail.take(ring + 1, grads.at[after, low])
    mail.post(across + 1, grads.at[after], grads.at[after], here.line(0, 1))
    copies.append(out(after, 1))
    mail.take(ring + 2, grads.at[before, high])
    mail.post(across + 2, grads.at[before], grads.at[before], here.line(0, 1))
    copies.append(out(before, 2))
    for n, at in enumerate((low, high)):
        mail.take(ring + 4 + n, grads.at[far, at])
        mail.post(across + 3 + n, grads.at[far, at], grads.at[far, at], here.line(0, 1))
    copies.append(out(far, 3))
    for n, dy in enumerate((0, 1, -1, 2)):
        c = here.cols(dy, 1)
        if n < 3:
            mail.take(across + n, grads.at[c])
        else:
            mail.take(across + 3, grads.at[c, low])
            mail.take(across + 4, grads.at[c, high])
        copies.append(out(c, 4 + n))
    for copy in copies:
        copy.wait()
    mail.drain()


def forward_layer(cols, live, features, adj, weight, bias, upstream):
    rows, slots, size, _ = adj.shape
    per, _, width = features.shape
    piece = per * size
    blocks = lax.axis_size("row") * piece // size
    pieces = lax.axis_size("col")
    vmem, anywhere = pl.BlockSpec(memory_space=pltpu.VMEM), pl.BlockSpec(memory_space=pl.ANY)
    smem = pl.BlockSpec(memory_space=pltpu.SMEM)
    return pl.pallas_call(
        forward_body,
        out_shape=(
            jax.ShapeDtypeStruct((piece, width), BF16),
            jax.ShapeDtypeStruct((SPACE * pieces, piece, width), BF16),
            jax.ShapeDtypeStruct((width, width), F32),
            jax.ShapeDtypeStruct((8, width), F32),
        ),
        in_specs=[smem, smem] + [anywhere] * 5,
        out_specs=(vmem, anywhere, vmem, vmem),
        scratch_shapes=[
            pltpu.VMEM((blocks + 1, size, width), BF16),
            pltpu.VMEM(adj.shape, BF16),
            pltpu.VMEM(weight.shape, BF16),
            pltpu.VMEM(bias.shape, F32),
            pltpu.VMEM(upstream.shape, BF16),
            pltpu.VMEM((4, piece, width), BF16),
            pltpu.VMEM((4, piece, width), BF16),
            pltpu.VMEM((4, piece, width), F32),
            pltpu.VMEM((3, piece, width), BF16),
            pltpu.VMEM((6, piece // 2, width), BF16),
            pltpu.VMEM((pieces, piece, width), BF16),
            pltpu.SemaphoreType.DMA((FORWARD_MAIL,)),
            pltpu.SemaphoreType.DMA((FORWARD_MAIL,)),
            pltpu.SemaphoreType.DMA((4,)),
            pltpu.SemaphoreType.DMA((8,)),
            pltpu.SemaphoreType.DMA((4,)),
        ],
        compiler_params=pltpu.CompilerParams(
            collective_id=0, has_side_effects=True, vmem_limit_bytes=56 << 20
        ),
        name="forward_layer",
    )(cols, live, features, adj, weight, bias, upstream)


PARTS = 4
SPACE = 16


def backward_body(
    cols_ref, live_ref, adj_hbm, grad_hbm, acc, adj, grad, in_sem
):
    rows, slots, size, _ = adj.shape
    blocks = acc.shape[0] - 1
    step = rows // PARTS

    def fetch(n):
        at = pl.ds(n * step, step)
        return (
            pltpu.make_async_copy(adj_hbm.at[at], adj.at[at], in_sem.at[0, n]),
            pltpu.make_async_copy(grad_hbm.at[at], grad.at[at], in_sem.at[1, n]),
        )

    for n in range(PARTS):
        for copy in fetch(n):
            copy.start()

    @pl.loop(0, blocks)
    def _(j):
        acc[j] = jnp.zeros_like(acc[j])

    @pl.loop(0, PARTS)
    def _(n):
        for copy in fetch(n):
            copy.wait()
        for u in range(step):
            i = n * step + u
            for k in range(slots):
                j = jnp.where(k < live_ref[0, i], cols_ref[k, 0, i], blocks)
                acc[j] += dot(adj[i, k], grad[i], ((0,), (0,)))


def backward_product(cols, live, adj, grad, blocks):
    rows, slots, size, _ = adj.shape
    width = grad.shape[2]
    vmem, smem, anywhere = pl.BlockSpec(memory_space=pltpu.VMEM), pl.BlockSpec(memory_space=pltpu.SMEM), pl.BlockSpec(memory_space=pl.ANY)
    return pl.pallas_call(
        backward_body,
        out_shape=jax.ShapeDtypeStruct((blocks + 1, size, width), F32),
        in_specs=[smem, smem, anywhere, anywhere],
        out_specs=vmem,
        scratch_shapes=[
            pltpu.VMEM(adj.shape, BF16),
            pltpu.VMEM((rows, size, width), BF16),
            pltpu.SemaphoreType.DMA((2, PARTS)),
        ],
        compiler_params=pltpu.CompilerParams(vmem_limit_bytes=40 << 20),
        name="backward_product",
    )(cols, live, adj, grad)


SCATTER_MAIL = 60
LINE_MAIL, SLICE_MAIL = 7, 3
BACK_MAIL = SCATTER_MAIL + 2 * LINE_MAIL + 3 * SLICE_MAIL


def back_body(
    sums_ref, wpart_ref, bpart_ref, feature_grad_ref, wgrad_ref, bgrad_ref,
    rx, tx, stage, w_out, w_in, x_out, x_in, z_in, slab, sent, came,
):
    here = Place()
    mail = Mail(here, sent, came)
    size = sums_ref.shape[1]
    nx = w_out.shape[0]
    slice_rows = wpart_ref.shape[0] // nx
    thin = slice_rows // RING
    peers = [here.plane(*at) for at in ((0, 1), (0, -1), (0, 2), (1, 0), (-1, 0), (2, 0))]
    peers += [(here.row, (here.col + d) % nx) for d in range(1, nx)]
    barrier = greet(peers)
    for d in range(1, nx):
        c = (here.col + d) % nx
        w_out[c, :slice_rows] = wpart_ref[pl.ds(c * slice_rows, slice_rows), :]
        w_out[c, slice_rows:] = bpart_ref[...]
    w_in[here.col, :slice_rows] = wpart_ref[pl.ds(here.col * slice_rows, slice_rows), :]
    w_in[here.col, slice_rows:] = bpart_ref[...]
    pl.semaphore_wait(*barrier)
    base = SCATTER_MAIL
    for d in range(1, nx):
        c = (here.col + d) % nx
        mail.post(base + d - 1, w_out.at[c], w_in.at[here.col], (here.row, c))

    def number(f, slot, kind):
        return f * 30 + slot * 6 + kind

    def to(f, slot, d):
        return here.plane(*(flavour(f, d, 0) if slot < 4 else flavour(f, 0, d)))

    def source(f, slot, d, b):
        if slot < 4:
            return sums_ref.at[here.rows(*flavour(f, d, OFFSETS[slot])) * 4 + 2 * f + b]
        return stage.at[f, OFFSETS.index(d), b]

    def send(f, slot, kind, d, b):
        n = number(f, slot, kind)
        src = tx.at[n]
        tx[n] = source(f, slot, 2 if kind < 2 else d, b)[...].astype(BF16)
        mail.post(n, src, rx.at[n], to(f, slot, d))

    def first(f, slot):
        send(f, slot, 0, 1, 0)
        send(f, slot, 1, -1, 1)

    def direct(f, slot):
        send(f, slot, 2, 1, 1)
        send(f, slot, 3, -1, 0)

    def onward(f, slot):
        for kind, d, b in ((0, 1, 0), (1, -1, 1)):
            mail.take(number(f, slot, kind), rx.at[number(f, slot, kind)])
            n = number(f, slot, 4 + kind)
            tx[n] = (source(f, slot, d, b)[...].astype(F32) + rx[number(f, slot, kind)].astype(F32)).astype(BF16)
            mail.post(n, tx.at[n], rx.at[n], to(f, slot, d))

    def total(f, slot, b):
        result = source(f, slot, 0, b)[...].astype(F32)
        for kind in ((4, 3) if b == 0 else (2, 5)):
            n = number(f, slot, kind)
            mail.take(n, rx.at[n])
            result = result + rx[n].astype(F32)
        return result

    both = (0, 1)

    def finish(slot):
        for f in both:
            for b in (0, 1):
                stage[f, slot, b] = total(f, slot, b)

    second = base + nx - 1
    third = second + SLICE_MAIL
    fourth = third + SLICE_MAIL
    fifth = fourth + SLICE_MAIL

    def added(parts, count):
        got = parts[0]
        for n in range(1, count):
            got = got + parts[n]
        return got

    def column_sums():
        for d in range(1, nx):
            mail.take(base + d - 1, w_in.at[(here.col + nx - d) % nx])
        got = added(w_in, nx)
        for n in range(RING):
            x_out[n, :thin] = got[n * thin : (n + 1) * thin]
            x_out[n, thin:] = got[slice_rows:]
        x_in[here.x] = x_out[here.x]
        for d in range(1, RING):
            mail.post(second + d - 1, x_out.at[(here.x + d) % RING], x_in.at[here.x], here.plane(0, d))

    def x_sums():
        for d in range(1, RING):
            mail.take(second + d - 1, x_in.at[(here.x + RING - d) % RING])
        z_in[here.z] = added(x_in, RING)
        for d in range(1, RING):
            mail.post(third + d - 1, z_in.at[here.z], z_in.at[here.z], here.plane(d, 0))

    def z_sums():
        for d in range(1, RING):
            mail.take(third + d - 1, z_in.at[(here.z + RING - d) % RING])
        got = added(z_in, RING)
        bgrad_ref[...] = jnp.sum(got[thin:], axis=0, keepdims=True)
        slab[here.x] = got[:thin]
        for d in range(1, RING):
            mail.post(fourth + d - 1, slab.at[here.x], slab.at[here.x], here.plane(0, d))

    mine = pl.ds(here.col * slice_rows, slice_rows)

    def spread():
        for d in range(1, RING):
            mail.take(fourth + d - 1, slab.at[(here.x + RING - d) % RING])
        for n in range(RING):
            wgrad_ref[pl.ds(here.col * slice_rows + n * thin, thin), :] = slab[n]
        for d in range(1, nx):
            mail.post(fifth + d - 1, wgrad_ref.at[mine], wgrad_ref.at[mine], (here.row, (here.col + d) % nx))

    def each(action, *slots):
        for slot in slots:
            for f in both:
                action(f, slot)

    each(first, 3)
    each(direct, 3)
    each(first, 1)
    each(onward, 3)
    each(first, 2)
    column_sums()
    each(onward, 1)
    each(direct, 1)
    x_sums()
    each(onward, 2)
    each(direct, 2)
    finish(3)
    each(first, 4)
    each(first, 0)
    z_sums()
    each(direct, 0)
    finish(1)
    finish(2)
    each(onward, 4)
    each(direct, 4)
    spread()
    each(onward, 0)
    finish(0)
    for f in both:
        for b in (0, 1):
            feature_grad_ref[pl.ds((2 * f + b) * size, size), :] = total(f, 4, b).astype(BF16)
    for d in range(1, nx):
        c = (here.col + nx - d) % nx
        mail.take(fifth + d - 1, wgrad_ref.at[pl.ds(c * slice_rows, slice_rows)])
    mail.drain()


def back_sums(sums, wpart, bpart, piece):
    _, size, width = sums.shape
    nx = lax.axis_size("col")
    slice_rows = width // nx
    vmem = pl.BlockSpec(memory_space=pltpu.VMEM)
    return pl.pallas_call(
        back_body,
        out_shape=(
            jax.ShapeDtypeStruct((piece, width), BF16),
            jax.ShapeDtypeStruct((width, width), F32),
            jax.ShapeDtypeStruct((1, width), F32),
        ),
        in_specs=[vmem, vmem, vmem],
        out_specs=(vmem, vmem, vmem),
        scratch_shapes=[
            pltpu.VMEM((SCATTER_MAIL, size, width), BF16),
            pltpu.VMEM((SCATTER_MAIL, size, width), BF16),
            pltpu.VMEM((2, 4, 2, size, width), F32),
            pltpu.VMEM((nx, slice_rows + EXTRA, width), F32),
            pltpu.VMEM((nx, slice_rows + EXTRA, width), F32),
            pltpu.VMEM((RING, slice_rows // RING + EXTRA, width), F32),
            pltpu.VMEM((RING, slice_rows // RING + EXTRA, width), F32),
            pltpu.VMEM((RING, slice_rows // RING + EXTRA, width), F32),
            pltpu.VMEM((RING, slice_rows // RING, width), F32),
            pltpu.SemaphoreType.DMA((BACK_MAIL,)),
            pltpu.SemaphoreType.DMA((BACK_MAIL,)),
        ],
        compiler_params=pltpu.CompilerParams(
            collective_id=1, has_side_effects=True, vmem_limit_bytes=24 << 20
        ),
        name="back_sums",
    )(sums, wpart, bpart)


def hand_over(*arrays):
    def body(*refs):
        for source, target in zip(refs[: len(arrays)], refs[len(arrays) :]):
            target[...] = source[...]

    vmem = pl.BlockSpec(memory_space=pltpu.VMEM)
    return pl.pallas_call(
        body,
        out_shape=tuple(jax.ShapeDtypeStruct(a.shape, a.dtype) for a in arrays),
        in_specs=[vmem] * len(arrays),
        out_specs=(vmem,) * len(arrays),
        compiler_params=pltpu.CompilerParams(vmem_limit_bytes=4 << 20),
        name="hand_over",
    )(*arrays)


def local(features, adjacency, block_cols, block_live, weight, bias, upstream):
    rows, _, slots, size, _ = adjacency.shape
    piece, width = features.shape
    adj = adjacency.reshape(rows, slots, size, size)
    blocks = piece * lax.axis_size("row") // size
    cols = block_cols.transpose(2, 1, 0)
    live = block_live.reshape(1, rows)
    act, grads, wpart, bpart = forward_layer(
        cols, live, features.reshape(piece // size, size, width), adj, weight, bias.reshape(1, width), upstream
    )
    sums = backward_product(cols, live, adj, grads.reshape(SPACE * rows, size, width), blocks)
    act, feature_grad, wgrad, bgrad = hand_over(act, *back_sums(sums, wpart, bpart, piece))
    return act, feature_grad, wgrad, bgrad.reshape(width)


def solution(mesh):
    placed = (
        P(("col", "row"), None),
        P("row", "col", None, None, None),
        P("row", "col", None),
        P("row", "col"),
        P(),
        P(),
        P(("row", "col"), None),
    )
    return jax.shard_map(
        local,
        mesh=mesh,
        in_specs=placed,
        out_specs=(P(("row", "col"), None), P(("col", "row"), None), P(), P()),
        check_vma=False,
    )
```
